32 devices in a mesh: parts: 1, head: 32 (over z, y, x, core).
Axes of the slice: x: 2, y: 2, z: 4, core: 2. Of those that a mesh axis runs over, the one named last changes fastest.
Arguments:
- queries: bfloat16 [8, 2048, 2048], P('parts', 'head'), may hold values from -6 to 6
- keys: bfloat16 [8, 2048, 2048], P('parts', 'head'), may hold values from -6 to 6
- values: bfloat16 [8, 2048, 2048], P('parts', 'head'), may hold values from -6 to 6
- slot_positions: int32 [8, 2048], P('parts', 'head'), may hold values from 0 to 2047, each once within a row
- counts: int32 [8], P('parts'), may hold values from 16 to 2048, as said below
- timesteps: int32 [8], P('parts'), may hold values from 0 to 999
- labels: int32 [8], P('parts'), may hold values from 0 to 127
- time_weight: bfloat16 [256, 4096], replicated, may hold values from -0.375 to 0.375
- norm_gain: float32 [2048], replicated, may hold values from 0.25 to 1.75
- gate_weight: bfloat16 [2048, 8192], P(None, 'head'), may hold values from -0.125 to 0.125
- up_weight: bfloat16 [2048, 8192], P(None, 'head'), may hold values from -0.125 to 0.125
- down_weight: bfloat16 [8192, 2048], P('head'), may hold values from -0.0625 to 0.0625
- class_weight: bfloat16 [2048, 128], replicated, may hold values from -3 to 3
- class_bias: float32 [128], replicated, may hold values from -5 to 112
Outputs:
- attention: bfloat16 [256, 2048, 64], P(('parts', 'head'))
- guidance: float32 [8, 128, 2048], P('parts', 'head')
The draws below stay inside these ranges and needn't reach their ends.
Inputs may be any that keep to these rules, and one draw needn't show every extreme that they name: `counts`: multiples of 16; in every part one shower has exactly 2048. `slot_positions`: each shower's row is a permutation of 0 to 2047.
All inputs are finite; a program needn't handle non-finite values.
Results may differ from the reference program's by a relative error of at most 0.01.
The reference program's roundings to bfloat16 on the way count: a program that leaves them out, or rounds other values in their place, can miss the bound.
Values may be sent and summed in bfloat16 or wider, within the bound.
A program may use at most 192 MiB of HBM per device.

```python
import math
import jax
import jax.numpy as jnp
from jax import lax

HEADS = 32
HD = 64
CD = 2048
FF = 8192
L = 2048
SH = 8
POOL = 16
FREQ = 256
NT = 1000
CLASSES = 128
PAIRS = 256
WP = 128
ROWS = 1024


def drawn_fields(key):
    field_shape = (SH, L, HEADS * HD)
    query_base = jnp.clip(jax.random.normal(jax.random.fold_in(key, 11), field_shape, jnp.float32), -6.0, 6.0)
    key_base = jnp.clip(jax.random.normal(jax.random.fold_in(key, 12), field_shape, jnp.float32), -6.0, 6.0)
    return (query_base, key_base)


def draw_queries(key, part):
    return drawn_fields(key)[0].astype(jnp.bfloat16)


def draw_keys(key, part):
    return drawn_fields(key)[1].astype(jnp.bfloat16)


def draw_counts(key, part):
    units = jax.random.randint(jax.random.fold_in(key, 21), (SH,), 1, L // POOL + 1)
    fullest = jax.random.randint(jax.random.fold_in(key, 22), (), 0, SH)
    units = jnp.where(jnp.arange(SH) == fullest, L // POOL, units)
    return (units * POOL).astype(jnp.int32)


def draw_class_bias(key, part):
    biases = jnp.clip(jax.random.normal(jax.random.fold_in(key, 31), (CLASSES,), jnp.float32), -5.0, 5.0)
    return biases


def touch_ends(result, key, least, top_value):
    extent = result.shape
    index_at = [jax.random.randint(jax.random.fold_in(key, axis), (), 0, extent[axis]) for axis in range(len(extent))]
    result = result.at[tuple(index_at)].set(least)
    longest = extent.index(max(extent))
    index_at[longest] = (index_at[longest] + 1) % extent[longest]
    return result.at[tuple(index_at)].set(top_value)


def level_of(own_key, extent, cuts, smallest, top_value):
    def one(position, parts):
        draws = jax.random.uniform(jax.random.fold_in(jax.random.fold_in(own_key, 6), position), (parts,), jnp.float32, smallest / len(cuts), top_value / len(cuts))
        return jnp.repeat(jnp.exp(draws), extent[position] // parts).reshape((-1,) + (1,) * (len(extent) - position - 1))

    level = one(*cuts[0])
    for cut in cuts[1:]:
        level = level * one(*cut)
    return level


def scatter_about(key, dims, deviation, limit, pieces=(), kind=jnp.bfloat16):
    values = deviation * jax.random.normal(key, dims, jnp.float32)
    if pieces:
        values = values * level_of(key, dims, pieces, -0.22, 0.18)
    return jnp.clip(values, -limit, limit).astype(kind)


def setup_inputs(seed: int = 0, part: int = 0) -> dict:
    seeds = jax.random.split(jax.random.key(seed), 15)
    part_splits = jax.random.split(jax.random.fold_in(seeds[14], part), 15)
    queries = draw_queries(jax.random.fold_in(jax.random.fold_in(seeds[14], part), 71), part)
    keys = draw_keys(jax.random.fold_in(jax.random.fold_in(seeds[14], part), 71), part)
    values = scatter_about(part_splits[2], (SH, L, CD), 1.0, 6.0, ((1, 32),))
    slot_positions = jax.vmap(lambda own: jax.random.permutation(own, L))(jax.random.split(part_splits[3], SH)).reshape((SH, L)).astype(jnp.int32)
    counts = draw_counts(jax.random.fold_in(jax.random.fold_in(seeds[14], part), 71), part)
    timesteps = touch_ends(jax.random.randint(part_splits[5], (SH,), 0, NT), jax.random.fold_in(part_splits[5], 1), 0, NT - 1).astype(jnp.int32)
    labels = touch_ends(jax.random.randint(part_splits[6], (SH,), 0, CLASSES), jax.random.fold_in(part_splits[6], 1), 0, CLASSES - 1).astype(jnp.int32)
    time_weight = scatter_about(seeds[7], (FREQ, 2 * CD), FREQ ** -0.5, 0.375)
    norm_gain = jnp.clip(1.0 + 0.15 * jax.random.normal(seeds[8], (CD,), jnp.float32), 0.25, 1.75)
    gate_weight = scatter_about(seeds[9], (CD, FF), CD ** -0.5, 0.125, ((1, 32),))
    up_weight = scatter_about(seeds[10], (CD, FF), CD ** -0.5, 0.125, ((1, 32),))
    down_weight = scatter_about(seeds[11], (FF, CD), FF ** -0.5, 0.0625, ((0, 32),))
    class_weight = scatter_about(seeds[12], (CD, CLASSES), 0.5, 3.0)
    class_bias = draw_class_bias(jax.random.fold_in(seeds[14], 71), part)
    return {"queries": queries, "keys": keys, "values": values, "slot_positions": slot_positions, "counts": counts, "timesteps": timesteps, "labels": labels, "time_weight": time_weight, "norm_gain": norm_gain, "gate_weight": gate_weight, "up_weight": up_weight, "down_weight": down_weight, "class_weight": class_weight, "class_bias": class_bias}


epsilon = 1e-06

def sinusoid(steps):
    half_width = FREQ // 2
    frequency = jnp.exp(-math.log(10000.0) * jnp.arange(half_width, dtype=jnp.float32) / half_width)
    angles = steps.astype(jnp.float32)[:, None] * frequency[None, :]
    return jnp.concatenate([jnp.cos(angles), jnp.sin(angles)], axis=1)

def to_pairs(block):
    return block.reshape(SH, L, HEADS, HD).transpose(0, 2, 1, 3).reshape(PAIRS, L, HD)

def attend_pair(pair_data):
    query_rows, key_rows, value_rows, key_valid = pair_data
    scores = jnp.dot(query_rows, key_rows.T, preferred_element_type=jnp.float32) * HD ** (-0.5)
    scores = jnp.where(key_valid[None, :], scores, -jnp.inf)
    peak = lax.optimization_barrier(jnp.max(scores, axis=1, keepdims=True))
    exponent = jnp.exp(scores - peak)
    weights = (exponent / lax.optimization_barrier(jnp.sum(exponent, axis=1, keepdims=True))).astype(jnp.bfloat16)
    mixed = jnp.dot(weights, value_rows, preferred_element_type=jnp.float32)
    return (mixed * key_valid[:, None].astype(jnp.float32)).astype(jnp.bfloat16)

def reference(queries, keys, values, slot_positions, counts, timesteps, labels, time_weight, norm_gain, gate_weight, up_weight, down_weight, class_weight, class_bias):
    valid_slots = slot_positions < counts[:, None]
    pair_valid = jnp.repeat(valid_slots, HEADS, axis=0)
    attention = lax.map(attend_pair, (to_pairs(queries), to_pairs(keys), to_pairs(values), pair_valid))
    slot_flags = pair_valid.astype(jnp.float32)
    window_count = lax.optimization_barrier(jnp.sum(slot_flags.reshape(PAIRS, WP, POOL), axis=2))
    window_sum = lax.optimization_barrier(jnp.sum(attention.astype(jnp.float32).reshape(PAIRS, WP, POOL, HD), axis=2))
    pooled = (window_sum / jnp.maximum(window_count, 1.0)[:, :, None]).astype(jnp.bfloat16)
    pooled_rows = pooled.reshape(SH, HEADS, WP, HD).transpose(0, 2, 1, 3).reshape(SH, WP, CD).astype(jnp.float32)
    row_count = window_count.reshape(SH, HEADS, WP)[:, 0, :]
    embedding = sinusoid(timesteps).astype(jnp.bfloat16)
    modulation = jnp.dot(embedding, time_weight, preferred_element_type=jnp.float32)
    shifts = modulation[:, None, :CD]
    scales = 1.0 + modulation[:, None, CD:]
    inverse_rms = lax.rsqrt(lax.optimization_barrier(jnp.mean(pooled_rows * pooled_rows, axis=2, keepdims=True)) + epsilon)
    unit_rows = pooled_rows * inverse_rms
    normed = (unit_rows * norm_gain * scales + shifts).astype(jnp.bfloat16).reshape(ROWS, CD)
    gate_out = jnp.dot(normed, gate_weight, preferred_element_type=jnp.float32)
    up_out = jnp.dot(normed, up_weight, preferred_element_type=jnp.float32)
    activated = jax.nn.silu(gate_out)
    hidden = (activated * up_out).astype(jnp.bfloat16)
    mlp_out = jnp.dot(hidden, down_weight, preferred_element_type=jnp.float32).reshape(SH, WP, CD)
    shower_counts = counts.astype(jnp.float32)
    features = lax.optimization_barrier(jnp.sum(row_count[:, :, None] * (pooled_rows + mlp_out), axis=1)) / shower_counts[:, None]
    class_matrix = class_weight.astype(jnp.float32)
    logits = jnp.dot(features, class_matrix, precision=lax.Precision.HIGHEST) + class_bias
    exponent = jnp.exp(logits - lax.optimization_barrier(jnp.max(logits, axis=1, keepdims=True)))
    probability = exponent / lax.optimization_barrier(jnp.sum(exponent, axis=1, keepdims=True))
    target = (labels[:, None] == jnp.arange(CLASSES, dtype=jnp.int32)[None, :]).astype(jnp.float32)
    feature_grad = jnp.dot(target - probability, class_matrix.T, precision=lax.Precision.HIGHEST)
    row_grads = row_count[:, :, None] / shower_counts[:, None, None] * feature_grad[:, None, :]
    hidden_grad = jnp.dot(row_grads.astype(jnp.bfloat16).reshape(ROWS, CD), down_weight.T, preferred_element_type=jnp.float32)
    sigmoid_gate = jax.nn.sigmoid(gate_out)
    gate_grad = (hidden_grad * up_out * sigmoid_gate * (1.0 + gate_out * (1.0 - sigmoid_gate))).astype(jnp.bfloat16)
    up_grad = (hidden_grad * activated).astype(jnp.bfloat16)
    normed_grad = jnp.dot(gate_grad, gate_weight.T, preferred_element_type=jnp.float32) + jnp.dot(up_grad, up_weight.T, preferred_element_type=jnp.float32)
    unit_grad = normed_grad.reshape(SH, WP, CD) * norm_gain * scales
    pooled_grad = inverse_rms * (unit_grad - unit_rows * lax.optimization_barrier(jnp.mean(unit_grad * unit_rows, axis=2, keepdims=True)))
    guidance = WP * (row_grads + pooled_grad)
    return (attention, guidance)
```

```python
import functools
import math

import jax
import jax.numpy as jnp
from jax import lax
from jax.experimental import pallas as pl
from jax.experimental.pallas import tpu as pltpu
from jax.sharding import PartitionSpec as P

HEADS = 32
POOL = 16
QTILE = 256
AHEAD = 4
STRIDE = 11
MESH = pl.DeviceIdType.MESH

epsilon = 1e-06
HIGHEST = lax.Precision.HIGHEST


def sinusoid(steps, embed_width):
    half_width = embed_width // 2
    frequency = jnp.exp(-math.log(10000.0) * jnp.arange(half_width, dtype=jnp.float32) / half_width)
    angles = steps.astype(jnp.float32)[:, None] * frequency[None, :]
    return jnp.concatenate([jnp.cos(angles), jnp.sin(angles)], axis=1)


def greet_all(n, me):
    barrier = pltpu.get_barrier_semaphore()

    def greet(k, carry):
        pl.semaphore_signal(
            barrier, inc=1, device_id={"head": lax.rem(me + k, n)}, device_id_type=MESH
        )
        return carry

    lax.fori_loop(1, n, greet, 0)
    pl.semaphore_wait(barrier, n - 1)


def exchange_attend_kernel(
    n, head_dim, stride, q, k, v, pos, cnt, att, pooled, everywhere,
    qb, kb, vb, key_turned, mixed_in, att_held, bias_row, valid_col,
    send_sem, recv_sem, pos_send, pos_recv, out_sem,
):
    me = lax.axis_index("head")
    showers, rows, width = q.shape
    chunks, length, lanes = qb.shape
    cols = chunks * lanes
    groups = width // cols
    heads = lanes // head_dim
    per_lane_row = lanes // rows
    fields = ((q, qb), (k, kb), (v, vb))
    greet_all(n, me)

    def block_of(field, dst, c):
        start = pl.multiple_of((dst % groups) * cols + c * lanes, lanes)
        return field.at[dst // groups, :, pl.ds(start, lanes)]

    def slot_of(held, src, c):
        return held.at[c, pl.ds(pl.multiple_of(src * rows, rows), rows), :]

    def send_pos(step, carry):
        pltpu.make_async_remote_copy(
            src_ref=pos,
            dst_ref=everywhere.at[me],
            send_sem=pos_send,
            recv_sem=pos_recv,
            device_id={"head": lax.rem(me + step, n)},
            device_id_type=MESH,
        ).start()
        return carry

    pltpu.make_async_copy(pos, everywhere.at[me], pos_recv).start()
    lax.fori_loop(1, n, send_pos, 0)

    def send_chunk(c, carry):
        for i, (a, o) in enumerate(fields):
            pltpu.make_async_copy(block_of(a, me, c), slot_of(o, me, c), recv_sem.at[i, c]).start()

        def one(step, inner):
            dst = lax.rem(me + step * stride, n)
            for i, (a, o) in enumerate(fields):
                pltpu.make_async_remote_copy(
                    src_ref=block_of(a, dst, c),
                    dst_ref=slot_of(o, me, c),
                    send_sem=send_sem.at[i, c],
                    recv_sem=recv_sem.at[i, c],
                    device_id={"head": dst},
                    device_id_type=MESH,
                ).start()
            return inner

        lax.fori_loop(1, n, one, 0)
        return carry

    ahead = min(AHEAD, chunks)
    lax.fori_loop(0, ahead, send_chunk, 0)

    def wait_whole(ref, sem):
        pltpu.make_async_copy(ref, ref, sem).wait()

    wait_whole(everywhere, pos_recv)
    wait_whole(everywhere.at[pl.ds(0, n - 1)], pos_send)
    own = me // groups
    limit = cnt[pl.ds(own, 1), :]

    def mark(m, carry):
        place = everywhere[m * per_lane_row, pl.ds(own, 1), :]
        for i in range(1, per_lane_row):
            place = place + everywhere[m * per_lane_row + i, pl.ds(own, 1), :]
        valid = place < limit
        at = pl.ds(pl.multiple_of(m * lanes, lanes), lanes)
        bias_row[:, at] = jnp.where(valid, 0.0, -1e30)
        wide = jnp.broadcast_to(jnp.where(valid, 1.0, 0.0), (lanes, lanes))
        valid_col[at, :] = wide.T
        return carry

    lax.fori_loop(0, length // lanes, mark, 0)

    qtile = min(QTILE, length)
    kblock = min(512, length)
    lane = lax.broadcasted_iota(jnp.int32, (qtile, lanes), 1)
    windows = qtile // POOL
    window_row = lax.broadcasted_iota(jnp.int32, (windows, qtile), 0)
    window_slot = lax.broadcasted_iota(jnp.int32, (windows, qtile), 1)
    gather = jnp.where(window_slot // POOL == window_row, 1.0, 0.0).astype(jnp.bfloat16)
    factor = math.log2(math.e) * head_dim ** (-0.5)

    def chunk(c, carry):
        @pl.when(c + ahead < chunks)
        def _():
            send_chunk(c + ahead, 0)

        for i, (a, o) in enumerate(fields):
            wait_whole(o.at[c], recv_sem.at[i, c])

        def prepare(b, inner):
            at = pl.ds(pl.multiple_of(b * kblock, kblock), kblock)
            turned = kb[c, at, :].astype(jnp.float32).T
            row = lax.broadcasted_iota(jnp.int32, (lanes, kblock), 0)
            key_lane = lax.broadcasted_iota(jnp.int32, (kblock, lanes), 1)
            bias = bias_row[:, at]
            value = vb[c, at, :].astype(jnp.float32)
            for h in range(heads):
                spare = ((h + 1) % heads) * head_dim
                key_turned[h, 0:lanes, at] = turned.astype(jnp.bfloat16)
                key_turned[h, lanes : 2 * lanes, at] = jnp.where(row == spare, bias, turned).astype(
                    jnp.bfloat16
                )
                mixed_in[h, at, :] = jnp.where(key_lane == spare, 1.0, value).astype(jnp.bfloat16)
            return inner

        lax.fori_loop(0, length // kblock, prepare, 0)

        def tile(t, inner):
            at = pl.ds(pl.multiple_of(t * qtile, qtile), qtile)
            query = qb[c, at, :].astype(jnp.float32) * factor
            high = query.astype(jnp.bfloat16).astype(jnp.float32)
            low = query - high
            valid = valid_col[at, :]
            joined = None
            for h in range(heads):
                spare = ((h + 1) % heads) * head_dim
                inside = (lane >= h * head_dim) & (lane < (h + 1) * head_dim)
                both = jnp.concatenate(
                    [
                        jnp.where(inside, high, 0.0).astype(jnp.bfloat16),
                        jnp.where(inside, low, jnp.where(lane == spare, 1.0, 0.0)).astype(
                            jnp.bfloat16
                        ),
                    ],
                    axis=1,
                )
                scores = jnp.dot(both, key_turned[h], preferred_element_type=jnp.float32)
                peak = jnp.max(scores, axis=1, keepdims=True)
                weights = jnp.exp2(scores - peak).astype(jnp.bfloat16)
                result = jnp.dot(weights, mixed_in[h], preferred_element_type=jnp.float32)
                result = result * (valid / result[:, spare : spare + 1])
                joined = result if joined is None else jnp.where(inside, result, joined)
            turned = joined.T.astype(jnp.bfloat16)
            for h in range(heads):
                att_held[c * heads + h, :, at] = turned[h * head_dim : (h + 1) * head_dim, :]
            sums = jnp.dot(gather, joined.astype(jnp.bfloat16), preferred_element_type=jnp.float32)
            count = jnp.dot(gather, valid.astype(jnp.bfloat16), preferred_element_type=jnp.float32)
            pooled[
                pl.ds(pl.multiple_of(t * windows, windows), windows),
                pl.ds(pl.multiple_of(c * lanes, lanes), lanes),
            ] = (sums / jnp.maximum(count, 1.0)).astype(jnp.bfloat16)
            return inner

        lax.fori_loop(0, length // qtile, tile, 0)
        part = pl.ds(c * heads, heads)
        pltpu.make_async_copy(att_held.at[part], att.at[part], out_sem.at[c]).start()
        return carry

    lax.fori_loop(0, chunks, chunk, 0)

    def finish(c, carry):
        part = pl.ds(c * heads, heads)
        pltpu.make_async_copy(att_held.at[part], att.at[part], out_sem.at[c]).wait()
        for i, (a, o) in enumerate(fields):
            wait_whole(o.at[c, pl.ds(0, (n - 1) * rows)], send_sem.at[i, c])
        return carry

    lax.fori_loop(0, chunks, finish, 0)


def exchange_attend(n, q, k, v, pos, cnt, cols, head_dim):
    showers, rows, width = q.shape
    length = n * rows
    lanes = 2 * head_dim
    chunks = cols // lanes
    heads = cols // head_dim
    moving = pltpu.VMEM((chunks, length, lanes), jnp.bfloat16)
    return pl.pallas_call(
        functools.partial(exchange_attend_kernel, n, head_dim, STRIDE),
        out_shape=(
            jax.ShapeDtypeStruct((heads, head_dim, length), jnp.bfloat16),
            jax.ShapeDtypeStruct((length // POOL, cols), jnp.bfloat16),
            jax.ShapeDtypeStruct((n,) + pos.shape, pos.dtype),
        ),
        in_specs=[pl.BlockSpec(memory_space=pl.ANY)] * 3
        + [pl.BlockSpec(memory_space=pltpu.VMEM)] * 2,
        out_specs=[
            pl.BlockSpec(memory_space=pl.ANY),
            pl.BlockSpec(memory_space=pltpu.VMEM),
            pl.BlockSpec(memory_space=pltpu.VMEM),
        ],
        scratch_shapes=[
            moving,
            moving,
            moving,
            pltpu.VMEM((2, 2 * lanes, length), jnp.bfloat16),
            pltpu.VMEM((2, length, lanes), jnp.bfloat16),
            pltpu.VMEM((heads, head_dim, length), jnp.bfloat16),
            pltpu.VMEM((1, length), jnp.float32),
            pltpu.VMEM((length, lanes), jnp.float32),
            pltpu.SemaphoreType.DMA((3, chunks)),
            pltpu.SemaphoreType.DMA((3, chunks)),
            pltpu.SemaphoreType.DMA,
            pltpu.SemaphoreType.DMA,
            pltpu.SemaphoreType.DMA((chunks,)),
        ],
        compiler_params=pltpu.CompilerParams(
            collective_id=1, has_side_effects=True, vmem_limit_bytes=48 * 1024 * 1024
        ),
    )(q, k, v, pos, cnt)


def total_kernel(n, x, out, held, send_sem, recv_sem):
    me = lax.axis_index("head")
    greet_all(n, me)

    def copy_of(step):
        return pltpu.make_async_remote_copy(
            src_ref=x,
            dst_ref=held.at[step],
            send_sem=send_sem.at[step],
            recv_sem=recv_sem.at[step],
            device_id={"head": lax.rem(me + step, n)},
            device_id_type=MESH,
        )

    def begin(step, carry):
        copy_of(step).start()
        return carry

    def finish(step, carry):
        copy_of(step).wait()
        return carry

    held[0] = x[...]
    lax.fori_loop(1, n, begin, 0)
    lax.fori_loop(1, n, finish, 0)
    total = jnp.zeros(out.shape, jnp.float32)
    for source in range(n):
        total = total + held[lax.rem(me - source + n, n)]
    out[...] = total


def total_over(n, x):
    return pl.pallas_call(
        functools.partial(total_kernel, n),
        out_shape=jax.ShapeDtypeStruct(x.shape, jnp.float32),
        in_specs=[pl.BlockSpec(memory_space=pltpu.VMEM)],
        out_specs=pl.BlockSpec(memory_space=pltpu.VMEM),
        scratch_shapes=[
            pltpu.VMEM((n,) + x.shape, jnp.float32),
            pltpu.SemaphoreType.DMA((n,)),
            pltpu.SemaphoreType.DMA((n,)),
        ],
        compiler_params=pltpu.CompilerParams(collective_id=2, has_side_effects=True),
    )(x)


def scatter_plan(n, orders):
    plan = []
    for order in orders:
        stages = []
        kept = list(range(n))
        for position, bit in enumerate(order):
            away = [r for r in kept if (r >> bit) & 1]
            kept = [r for r in kept if not (r >> bit) & 1]
            following = order[position + 1] if position + 1 < len(order) else None
            if following is not None:
                kept.sort(key=lambda r: (1 - ((r >> following) & 1), r))
            away = [r ^ (1 << bit) for r in kept]
            away = [r for r in away]
            stages.append((bit, away, list(kept)))
        plan.append(stages)
    return plan


def reduce_kernel(n, plan, x, out, held, send_sem, recv_sem):
    me = lax.axis_index("head")
    bits = n.bit_length() - 1
    width = x.shape[2] // len(plan)
    bit_of = [(me // (1 << b)) % 2 for b in range(bits)]

    def flipped(r):
        result = me
        for b in range(bits):
            if (r >> b) & 1:
                result = result + (1 << b) * (1 - 2 * bit_of[b])
        return result

    barrier = pltpu.get_barrier_semaphore()
    for b in range(bits):
        pl.semaphore_signal(
            barrier, inc=1, device_id={"head": flipped(1 << b)}, device_id_type=MESH
        )
    pl.semaphore_wait(barrier, bits)

    def copy_of(stream, slot, bit, r):
        columns = pl.ds(stream * width, width)
        return pltpu.make_async_remote_copy(
            src_ref=x.at[flipped(r), :, columns],
            dst_ref=held.at[stream, slot],
            send_sem=send_sem.at[stream, slot],
            recv_sem=recv_sem.at[stream, slot],
            device_id={"head": flipped(1 << bit)},
            device_id_type=MESH,
        )

    stage_count = len(plan[0])
    slots = [0]
    for stage in range(stage_count):
        slots.append(slots[-1] + len(plan[0][stage][1]))
    everything = []
    for i in range(len(plan[0][0][1])):
        for stream, stages in enumerate(plan):
            bit, away, kept = stages[0]
            copy = copy_of(stream, i, bit, away[i])
            copy.start()
            everything.append(copy)
    for stage in range(stage_count):
        for i in range(len(plan[0][stage][1])):
            for stream, stages in enumerate(plan):
                bit, away, kept = stages[stage]
                slot = slots[stage] + i
                copy_of(stream, slot, bit, away[i]).wait_recv()
                columns = pl.ds(stream * width, width)
                chunk = flipped(kept[i])
                value = x[chunk, :, columns].astype(jnp.float32) + held[stream, slot].astype(
                    jnp.float32
                )
                if stage == stage_count - 1:
                    out[:, columns] = value
                    continue
                x[chunk, :, columns] = value.astype(jnp.bfloat16)
                next_bit, next_away, _ = stages[stage + 1]
                if kept[i] in next_away:
                    copy = copy_of(
                        stream,
                        slots[stage + 1] + next_away.index(kept[i]),
                        next_bit,
                        kept[i],
                    )
                    copy.start()
                    everything.append(copy)
    for copy in everything:
        copy.wait_send()


def reduce_kernel_entry(n, plan, x_ref, out, x, held, load_sem, send_sem, recv_sem):
    load = pltpu.make_async_copy(x_ref, x, load_sem)
    load.start()
    load.wait()
    reduce_kernel(n, plan, x, out, held, send_sem, recv_sem)


def reduce_over(n, x, orders):
    plan = scatter_plan(n, orders)
    chunks, rows, columns = x.shape
    streams = len(plan)
    return pl.pallas_call(
        functools.partial(reduce_kernel_entry, n, plan),
        out_shape=jax.ShapeDtypeStruct((rows, columns), jnp.float32),
        in_specs=[pl.BlockSpec(memory_space=pl.ANY)],
        out_specs=pl.BlockSpec(memory_space=pltpu.VMEM),
        scratch_shapes=[
            pltpu.VMEM(x.shape, x.dtype),
            pltpu.VMEM((streams, n, rows, columns // streams), x.dtype),
            pltpu.SemaphoreType.DMA,
            pltpu.SemaphoreType.DMA((streams, n)),
            pltpu.SemaphoreType.DMA((streams, n)),
        ],
        compiler_params=pltpu.CompilerParams(
            collective_id=3, has_side_effects=True, vmem_limit_bytes=40 * 1024 * 1024
        ),
    )(x)


def collect_kernel(n, orders, x, out, own_sem, send_sem, recv_sem):
    me = lax.axis_index("head")
    bits = n.bit_length() - 1
    height = x.shape[0] // len(orders)
    bit_of = [(me // (1 << b)) % 2 for b in range(bits)]

    def flipped(r):
        result = me
        for b in range(bits):
            if (r >> b) & 1:
                result = result + (1 << b) * (1 - 2 * bit_of[b])
        return result

    barrier = pltpu.get_barrier_semaphore()
    for b in range(bits):
        pl.semaphore_signal(
            barrier, inc=1, device_id={"head": flipped(1 << b)}, device_id_type=MESH
        )
    pl.semaphore_wait(barrier, bits)

    own = pltpu.make_async_copy(x, out.at[me], own_sem)
    own.start()
    everything = []

    def copy_of(stream, r, bit):
        rows = pl.ds(stream * height, height)
        return pltpu.make_async_remote_copy(
            src_ref=x.at[rows] if r == 0 else out.at[flipped(r), rows],
            dst_ref=out.at[flipped(r), rows],
            send_sem=send_sem.at[stream, r | (1 << bit)],
            recv_sem=recv_sem.at[stream, r | (1 << bit)],
            device_id={"head": flipped(1 << bit)},
            device_id_type=MESH,
        )

    def pass_on(stream, r, later):
        for bit in later:
            copy = copy_of(stream, r, bit)
            copy.start()
            everything.append(copy)

    for stream, order in enumerate(orders):
        pass_on(stream, 0, order)
    held = [[0] for _ in orders]
    for stage in range(bits):
        for i in range(1 << stage):
            for stream, order in enumerate(orders):
                bit = order[stage]
                r = held[stream][i]
                copy_of(stream, r, bit).wait_recv()
                pass_on(stream, r | (1 << bit), order[stage + 1 :])
        for stream, order in enumerate(orders):
            held[stream] += [r | (1 << order[stage]) for r in held[stream]]
    for copy in everything:
        copy.wait_send()
    own.wait()


def collect_over(n, x, orders):
    return pl.pallas_call(
        functools.partial(collect_kernel, n, orders),
        out_shape=jax.ShapeDtypeStruct((n,) + x.shape, x.dtype),
        in_specs=[pl.BlockSpec(memory_space=pl.ANY)],
        out_specs=pl.BlockSpec(memory_space=pl.ANY),
        scratch_shapes=[
            pltpu.SemaphoreType.DMA,
            pltpu.SemaphoreType.DMA((len(orders), n)),
            pltpu.SemaphoreType.DMA((len(orders), n)),
        ],
        compiler_params=pltpu.CompilerParams(collective_id=4, has_side_effects=True),
    )(x)


def body(
    queries,
    keys,
    values,
    slot_positions,
    counts,
    timesteps,
    labels,
    time_weight,
    norm_gain,
    gate_weight,
    up_weight,
    down_weight,
    class_weight,
    class_bias,
):
    devices = lax.axis_size("head")
    device_index = lax.axis_index("head")
    showers, local_length, model_width = queries.shape
    head_dim = model_width // HEADS
    pairs_here = showers * HEADS // devices
    length = local_length * devices
    windows = length // POOL
    per_device = windows // devices
    row_total = showers * windows
    cols = pairs_here * head_dim
    groups = model_width // cols

    lanes = 2 * head_dim
    per_lane_row = lanes // local_length
    positions = lax.dynamic_update_slice_in_dim(
        jnp.zeros((showers, lanes), jnp.int32),
        slot_positions,
        (device_index % per_lane_row) * local_length,
        1,
    )
    attention, pooled, position_rows = exchange_attend(
        devices,
        queries,
        keys,
        values,
        positions,
        jnp.broadcast_to(counts[:, None], (showers, lanes)),
        cols,
        head_dim,
    )
    place = jnp.sum(position_rows.reshape(length // lanes, per_lane_row, showers, lanes), axis=1)
    valid_all = (place < counts[None, :, None]).astype(jnp.float32)
    row_count = jnp.sum(
        valid_all.reshape(length // lanes, showers, per_lane_row, per_device, POOL), axis=4
    )
    row_count = row_count.transpose(0, 2, 1, 3).reshape(devices, showers, per_device)
    bits = devices.bit_length() - 1
    high = list(range(bits - 1, 2, -1))
    pooled_all = collect_over(devices, pooled, (high[::-1] + [2, 1, 0], high[::-1] + [1, 2, 0]))
    by_shower = (
        pooled_all.reshape(showers, groups, windows, cols)
        .transpose(0, 2, 1, 3)
        .reshape(row_total, model_width)
    )
    row_id = jnp.arange(row_total, dtype=jnp.int32)
    owner = row_id // (showers * per_device)
    shower_of = (row_id // per_device) % showers
    source = shower_of * windows + owner * per_device + row_id % per_device
    order = (source[:, None] == row_id[None, :]).astype(jnp.bfloat16)
    pooled_rows = jnp.dot(order, by_shower, preferred_element_type=jnp.float32)
    in_shower = shower_of[:, None] == jnp.arange(showers, dtype=jnp.int32)[None, :]
    flat_count = row_count.reshape(row_total)
    spread = in_shower.astype(jnp.float32)

    embedding = sinusoid(timesteps, time_weight.shape[0]).astype(jnp.bfloat16)
    modulation = jnp.dot(embedding, time_weight, preferred_element_type=jnp.float32)
    shifts = modulation[None, :, None, :model_width]
    scales = 1.0 + modulation[:, model_width:]
    gains = norm_gain * scales
    inverse_rms = lax.rsqrt(jnp.mean(pooled_rows * pooled_rows, axis=1, keepdims=True) + epsilon)

    def by_row(table):
        rows = jnp.broadcast_to(table[:, None, :], (showers, per_device, table.shape[1]))
        rows = lax.optimization_barrier(rows.reshape(1, showers * per_device, table.shape[1]))
        wide = jnp.broadcast_to(rows, (devices,) + rows.shape[1:])
        return wide.reshape(row_total, table.shape[1])

    unit_rows = pooled_rows * inverse_rms
    normed = (
        unit_rows * norm_gain * by_row(scales) + by_row(modulation[:, :model_width])
    ).astype(jnp.bfloat16)
    shower_counts = counts.astype(jnp.float32)
    class_matrix = class_weight.astype(jnp.float32)
    target = (
        labels[:, None] == jnp.arange(class_matrix.shape[1], dtype=jnp.int32)[None, :]
    ).astype(jnp.float32)
    gate_out = jnp.dot(normed, gate_weight, preferred_element_type=jnp.float32)
    up_out = jnp.dot(normed, up_weight, preferred_element_type=jnp.float32)
    activated = jax.nn.silu(gate_out)
    hidden = (activated * up_out).astype(jnp.bfloat16)
    weigh = (spread * flat_count[:, None]).astype(jnp.bfloat16)
    hidden_sum = lax.dot_general(
        weigh, hidden, (((0,), (0,)), ((), ())), preferred_element_type=jnp.float32
    )
    pooled_sum = lax.dot_general(
        weigh,
        pooled_rows.astype(jnp.bfloat16),
        (((0,), (0,)), ((), ())),
        preferred_element_type=jnp.float32,
    )
    mlp_sum = jnp.dot(hidden_sum, down_weight.astype(jnp.float32), precision=HIGHEST)
    partial_logits = jnp.dot(mlp_sum, class_matrix, precision=HIGHEST)
    logit_sum = total_over(devices, partial_logits) + jnp.dot(
        pooled_sum, class_matrix, precision=HIGHEST
    )
    logits = logit_sum / shower_counts[:, None] + class_bias
    exponent = jnp.exp(logits - jnp.max(logits, axis=1, keepdims=True))
    probability = exponent / jnp.sum(exponent, axis=1, keepdims=True)
    feature_grad = jnp.dot(target - probability, class_matrix.T, precision=HIGHEST)
    row_share = row_count / shower_counts[None, :, None]
    row_grads = row_share.reshape(row_total, 1) * by_row(feature_grad)
    hidden_grad = jnp.dot(
        row_grads.astype(jnp.bfloat16), down_weight.T, preferred_element_type=jnp.float32
    )
    sigmoid_gate = jax.nn.sigmoid(gate_out)
    gate_grad = (
        hidden_grad * up_out * sigmoid_gate * (1.0 + gate_out * (1.0 - sigmoid_gate))
    ).astype(jnp.bfloat16)
    up_grad = (hidden_grad * activated).astype(jnp.bfloat16)
    normed_grad = (
        jnp.dot(gate_grad, gate_weight.T, preferred_element_type=jnp.float32)
        + jnp.dot(up_grad, up_weight.T, preferred_element_type=jnp.float32)
    ).astype(jnp.bfloat16)
    rows_here = showers * per_device
    normed_grad = reduce_over(
        devices,
        normed_grad.reshape(devices, rows_here, model_width),
        ([0, 1, 2] + high, [0, 2, 1] + high),
    )

    def own_rows(table):
        return lax.dynamic_slice_in_dim(table, device_index * rows_here, rows_here, 0)

    def shower_rows(table):
        wide = jnp.broadcast_to(table[:, None, :], (showers, per_device, table.shape[1]))
        return wide.reshape(rows_here, table.shape[1])

    own_pooled = own_rows(pooled_rows)
    own_inverse = lax.rsqrt(jnp.mean(own_pooled * own_pooled, axis=1, keepdims=True) + epsilon)
    own_units = own_pooled * own_inverse
    own_share = lax.dynamic_index_in_dim(row_share, device_index, 0, keepdims=False)
    own_row_grads = (own_share[:, :, None] * feature_grad[:, None, :]).reshape(
        rows_here, model_width
    )
    unit_grad = normed_grad * norm_gain * shower_rows(scales)
    pooled_grad = own_inverse * (
        unit_grad - own_units * jnp.mean(unit_grad * own_units, axis=1, keepdims=True)
    )
    guidance = windows * (own_row_grads + pooled_grad)
    return (attention.transpose(0, 2, 1), guidance.reshape(showers, per_device, model_width))


def solution(mesh):
    in_specs = (
        P("parts", "head", None),
        P("parts", "head", None),
        P("parts", "head", None),
        P("parts", "head"),
        P("parts"),
        P("parts"),
        P("parts"),
        P(),
        P(),
        P(None, "head"),
        P(None, "head"),
        P("head", None),
        P(),
        P(),
    )
    out_specs = (P(("parts", "head"), None, None), P("parts", "head", None))
    return jax.shard_map(body, mesh=mesh, in_specs=in_specs, out_specs=out_specs, check_vma=False)
```

```python
import functools
import math

import jax
import jax.numpy as jnp
from jax import lax
from jax.experimental import pallas as pl
from jax.experimental.pallas import tpu as pltpu
from jax.sharding import PartitionSpec as P

HEADS = 32
POOL = 16
QTILE = 256
AHEAD = 2
STRIDE = 11
VMEM_MIB = 60
MESH = pl.DeviceIdType.MESH

epsilon = 1e-06


def sinusoid(steps, embed_width):
    half_width = embed_width // 2
    frequency = jnp.exp(-math.log(10000.0) * jnp.arange(half_width, dtype=jnp.float32) / half_width)
    angles = steps.astype(jnp.float32)[:, None] * frequency[None, :]
    return jnp.concatenate([jnp.cos(angles), jnp.sin(angles)], axis=1)


def greet_all(n, me):
    barrier = pltpu.get_barrier_semaphore()

    def greet(k, carry):
        pl.semaphore_signal(
            barrier, inc=1, device_id={"head": lax.rem(me + k, n)}, device_id_type=MESH
        )
        return carry

    lax.fori_loop(1, n, greet, 0)
    pl.semaphore_wait(barrier, n - 1)


def scatter_plan(n, orders):
    plan = []
    for order in orders:
        stages = []
        kept = list(range(n))
        for position, bit in enumerate(order):
            kept = [r for r in kept if not (r >> bit) & 1]
            following = order[position + 1] if position + 1 < len(order) else None
            if following is not None:
                kept.sort(key=lambda r: (1 - ((r >> following) & 1), r))
            away = [r ^ (1 << bit) for r in kept]
            stages.append((bit, away, list(kept)))
        plan.append(stages)
    return plan


def split_dot(x, matrix, contract):
    high = x.astype(jnp.bfloat16).astype(jnp.float32)
    middle = (x - high).astype(jnp.bfloat16).astype(jnp.float32)
    low = x - high - middle
    parts = jnp.concatenate([high, middle, low], axis=0).astype(jnp.bfloat16)
    result = lax.dot_general(
        parts, matrix, (((1,), (contract,)), ((), ())), preferred_element_type=jnp.float32
    )
    rows = x.shape[0]
    return result[:rows] + result[rows : 2 * rows] + result[2 * rows :]


def block_kernel(
    n, head_dim, plan, orders,
    q, k, v, pos, cnt, labels, emb, gain, bias, time_hbm, gate_hbm, up_hbm, down_hbm, class_hbm,
    att, guidance,
    qb, kb, vb, key_turned, mixed_in, att_held, bias_row, valid_col, everywhere,
    gathered, normed, gate, up, down, time_w, class_w,
    g_all, u_all, dg_all, du_all, count_col, shift_tab, scale_tab, logit_in, logit_out,
    own_pooled, own_total, x, held,
    send_sem, recv_sem, pos_send, pos_recv, out_sem, load_sem,
    ag_send, ag_recv, logit_send, logit_recv, rs_send, rs_recv,
):
    me = lax.axis_index("head")
    showers, rows, width = q.shape
    chunks, length, lanes = qb.shape
    cols = chunks * lanes
    groups = width // cols
    heads = lanes // head_dim
    per_lane_row = lanes // rows
    window_count = length // POOL
    per_device = window_count // n
    rows_here = showers * per_device
    row_total = showers * window_count
    bits = n.bit_length() - 1
    streams = len(orders)
    bit_of = [(me // (1 << b)) % 2 for b in range(bits)]
    fields = ((q, qb), (k, kb), (v, vb))

    def flipped(r):
        result = me
        for b in range(bits):
            if (r >> b) & 1:
                result = result + (1 << b) * (1 - 2 * bit_of[b])
        return result

    greet_all(n, me)

    def block_of(field, dst, c):
        start = pl.multiple_of((dst % groups) * cols + c * lanes, lanes)
        return field.at[dst // groups, :, pl.ds(start, lanes)]

    def slot_of(held, src, c):
        return held.at[c, pl.ds(pl.multiple_of(src * rows, rows), rows), :]

    def send_pos(step, carry):
        pltpu.make_async_remote_copy(
            src_ref=pos,
            dst_ref=everywhere.at[me],
            send_sem=pos_send,
            recv_sem=pos_recv,
            device_id={"head": lax.rem(me + step, n)},
            device_id_type=MESH,
        ).start()
        return carry

    pltpu.make_async_copy(pos, everywhere.at[me], pos_recv).start()
    lax.fori_loop(1, n, send_pos, 0)

    def send_chunk(c, carry):
        for i, (a, o) in enumerate(fields):
            pltpu.make_async_copy(block_of(a, me, c), slot_of(o, me, c), recv_sem.at[i, c]).start()

        def one(step, inner):
            dst = lax.rem(me + step * STRIDE, n)
            for i, (a, o) in enumerate(fields):
                pltpu.make_async_remote_copy(
                    src_ref=block_of(a, dst, c),
                    dst_ref=slot_of(o, me, c),
                    send_sem=send_sem.at[i, c],
                    recv_sem=recv_sem.at[i, c],
                    device_id={"head": dst},
                    device_id_type=MESH,
                ).start()
            return inner

        lax.fori_loop(1, n, one, 0)
        return carry

    ahead = min(AHEAD, chunks)
    lax.fori_loop(0, ahead, send_chunk, 0)

    loads = [
        pltpu.make_async_copy(a, o, load_sem.at[i])
        for i, (a, o) in enumerate(
            (
                (time_hbm, time_w),
                (gate_hbm, gate),
                (up_hbm, up),
                (down_hbm, down),
                (class_hbm, class_w),
            )
        )
    ]
    for load in loads:
        load.start()
    for load in loads:
        load.wait()
    modulation = jnp.dot(emb[...], time_w[...], preferred_element_type=jnp.float32)
    for s in range(showers):
        shift_tab[s] = modulation[s : s + 1, :width]
        scale_tab[s] = gain[...] * (1.0 + modulation[s : s + 1, width:])

    def wait_whole(ref, sem):
        pltpu.make_async_copy(ref, ref, sem).wait()

    wait_whole(everywhere, pos_recv)
    wait_whole(everywhere.at[pl.ds(0, n - 1)], pos_send)
    own = me // groups

    def valid_at(m, s):
        place = everywhere[m * per_lane_row, pl.ds(s, 1), :]
        for i in range(1, per_lane_row):
            place = place + everywhere[m * per_lane_row + i, pl.ds(s, 1), :]
        return place < cnt[pl.ds(s, 1), :]

    def mark(m, carry):
        valid = valid_at(m, own)
        at = pl.ds(pl.multiple_of(m * lanes, lanes), lanes)
        bias_row[:, at] = jnp.where(valid, 0.0, -1e30)
        wide = jnp.broadcast_to(jnp.where(valid, 1.0, 0.0), (lanes, lanes))
        valid_col[at, :] = wide.T
        return carry

    lax.fori_loop(0, length // lanes, mark, 0)

    per_row = lanes // POOL
    member = lax.broadcasted_iota(jnp.int32, (per_row, lanes), 0) == (
        lax.broadcasted_iota(jnp.int32, (per_row, lanes), 1) // POOL
    )

    def tally(m, carry):
        at = pl.ds(pl.multiple_of(m * per_row, per_row), per_row)
        for s in range(showers):
            picked = jnp.where(member & valid_at(m, s), 1.0, 0.0)
            count_col[s, at, :] = jnp.broadcast_to(
                jnp.sum(picked, axis=1, keepdims=True), (per_row, lanes)
            )
        return carry

    lax.fori_loop(0, length // lanes, tally, 0)

    height = window_count // streams

    def gather_copy(c, stream, r, bit):
        part = gathered.at[
            flipped(r),
            pl.ds(stream * height, height),
            pl.ds(pl.multiple_of(c * lanes, lanes), lanes),
        ]
        return pltpu.make_async_remote_copy(
            src_ref=part,
            dst_ref=part,
            send_sem=ag_send.at[c, stream, r | (1 << bit)],
            recv_sem=ag_recv.at[c, stream, r | (1 << bit)],
            device_id={"head": flipped(1 << bit)},
            device_id_type=MESH,
        )

    def gather_begin(c):
        for bit_at in range(bits):
            for stream, order in enumerate(orders):
                gather_copy(c, stream, 0, order[bit_at]).start()

    def had_before(order, stage):
        result = [0]
        for bit in order[:stage]:
            result += [r | (1 << bit) for r in result]
        return result

    def gather_relay(c, stage):
        for i in range(1 << stage):
            for stream, order in enumerate(orders):
                bit = order[stage]
                r = had_before(order, stage)[i]
                gather_copy(c, stream, r, bit).wait_recv()
                for later in order[stage + 1 :]:
                    gather_copy(c, stream, r | (1 << bit), later).start()

    def gather_sent(c):
        for stream, order in enumerate(orders):
            for stage, bit in enumerate(order):
                for r in had_before(order, stage):
                    gather_copy(c, stream, r, bit).wait_send()

    qtile = min(QTILE, length)
    tiles = length // qtile
    kblock = min(512, length)
    lane = lax.broadcasted_iota(jnp.int32, (qtile, lanes), 1)
    windows = qtile // POOL
    window_row = lax.broadcasted_iota(jnp.int32, (windows, qtile), 0)
    window_slot = lax.broadcasted_iota(jnp.int32, (windows, qtile), 1)
    pool = jnp.where(window_slot // POOL == window_row, 1.0, 0.0).astype(jnp.bfloat16)
    factor = math.log2(math.e) * head_dim ** (-0.5)

    def chunk(c, carry):
        @pl.when(c + ahead < chunks)
        def _():
            send_chunk(c + ahead, 0)

        for i, (a, o) in enumerate(fields):
            wait_whole(o.at[c], recv_sem.at[i, c])

        def prepare(b, inner):
            at = pl.ds(pl.multiple_of(b * kblock, kblock), kblock)
            turned = kb[c, at, :].astype(jnp.float32).T
            row = lax.broadcasted_iota(jnp.int32, (lanes, kblock), 0)
            key_lane = lax.broadcasted_iota(jnp.int32, (kblock, lanes), 1)
            bias = bias_row[:, at]
            value = vb[c, at, :].astype(jnp.float32)
            for h in range(heads):
                spare = ((h + 1) % heads) * head_dim
                key_turned[h, 0:lanes, at] = turned.astype(jnp.bfloat16)
                key_turned[h, lanes : 2 * lanes, at] = jnp.where(row == spare, bias, turned).astype(
                    jnp.bfloat16
                )
                mixed_in[h, at, :] = jnp.where(key_lane == spare, 1.0, value).astype(jnp.bfloat16)
            return inner

        lax.fori_loop(0, length // kblock, prepare, 0)

        def tile(t, inner):
            if chunks > 1:
                for stage in range(bits):

                    @pl.when((c > 0) & (t == tiles - bits + stage))
                    def _():
                        gather_relay(c - 1, stage)

            at = pl.ds(pl.multiple_of(t * qtile, qtile), qtile)
            query = qb[c, at, :].astype(jnp.float32) * factor
            high = query.astype(jnp.bfloat16).astype(jnp.float32)
            low = query - high
            valid = valid_col[at, :]
            joined = None
            for h in range(heads):
                spare = ((h + 1) % heads) * head_dim
                inside = (lane >= h * head_dim) & (lane < (h + 1) * head_dim)
                both = jnp.concatenate(
                    [
                        jnp.where(inside, high, 0.0).astype(jnp.bfloat16),
                        jnp.where(inside, low, jnp.where(lane == spare, 1.0, 0.0)).astype(
                            jnp.bfloat16
                        ),
                    ],
                    axis=1,
                )
                scores = jnp.dot(both, key_turned[h], preferred_element_type=jnp.float32)
                peak = jnp.max(scores, axis=1, keepdims=True)
                weights = jnp.exp2(scores - peak).astype(jnp.bfloat16)
                result = jnp.dot(weights, mixed_in[h], preferred_element_type=jnp.float32)
                result = result * (valid / result[:, spare : spare + 1])
                joined = result if joined is None else jnp.where(inside, result, joined)
            turned = joined.T.astype(jnp.bfloat16)
            for h in range(heads):
                att_held[c * heads + h, :, at] = turned[h * head_dim : (h + 1) * head_dim, :]
            sums = jnp.dot(pool, joined.astype(jnp.bfloat16), preferred_element_type=jnp.float32)
            count = jnp.dot(pool, valid.astype(jnp.bfloat16), preferred_element_type=jnp.float32)
            gathered[
                me,
                pl.ds(pl.multiple_of(t * windows, windows), windows),
                pl.ds(pl.multiple_of(c * lanes, lanes), lanes),
            ] = (sums / jnp.maximum(count, 1.0)).astype(jnp.bfloat16)
            return inner

        lax.fori_loop(0, tiles, tile, 0)
        gather_begin(c)
        part = pl.ds(c * heads, heads)
        pltpu.make_async_copy(att_held.at[part], att.at[part], out_sem.at[c]).start()
        return carry

    lax.fori_loop(0, chunks, chunk, 0)
    for stage in range(bits):
        gather_relay(chunks - 1, stage)

    def finish(c, carry):
        part = pl.ds(c * heads, heads)
        pltpu.make_async_copy(att_held.at[part], att.at[part], out_sem.at[c]).wait()
        for i, (a, o) in enumerate(fields):
            wait_whole(o.at[c, pl.ds(0, (n - 1) * rows)], send_sem.at[i, c])
        gather_sent(c)
        return carry

    def norm(s, carry):
        total = None
        for j in range(groups):
            part = gathered[s * groups + j].astype(jnp.float32)
            square = jnp.sum(part * part, axis=1, keepdims=True)
            total = square if total is None else total + square
        inverse = lax.rsqrt(total * (1.0 / width) + epsilon)
        at = pl.ds(pl.multiple_of(s * window_count, window_count), window_count)
        for j in range(groups):
            columns = pl.ds(j * cols, cols)
            part = gathered[s * groups + j].astype(jnp.float32)
            normed[at, columns] = (
                part * inverse * scale_tab[s, :, columns] + shift_tab[s, :, columns]
            ).astype(jnp.bfloat16)
        return carry

    lax.fori_loop(0, showers, norm, 0)

    big = min(512, row_total)

    def forward(b, carry):
        at = pl.ds(pl.multiple_of(b * big, big), big)
        part = normed[at, :]
        g_all[at, :] = jnp.dot(part, gate[...], preferred_element_type=jnp.float32)
        u_all[at, :] = jnp.dot(part, up[...], preferred_element_type=jnp.float32)
        return carry

    lax.fori_loop(0, row_total // big, forward, 0)

    hidden_sums = []
    for s in range(showers):
        at = pl.ds(s * window_count, window_count)
        g, u = g_all[at, :], u_all[at, :]
        sigma = 1.0 / (1.0 + jnp.exp(-g))
        active = g * sigma
        hidden = (active * u).astype(jnp.bfloat16).astype(jnp.float32)
        hidden_sums.append(jnp.sum(count_col[s][:, 0:1] * hidden, axis=0, keepdims=True))
        g_all[at, :] = active
        u_all[at, :] = u * sigma * (1.0 + g * (1.0 - sigma))
    mlp_sum = split_dot(jnp.concatenate(hidden_sums, axis=0), down[...], 0)
    logit_part = split_dot(mlp_sum, class_w[...], 0)
    own_sum = jnp.sum(
        count_col[own][:, 0:1] * gathered[me].astype(jnp.float32), axis=0, keepdims=True
    )
    own_class = class_w[pl.ds(pl.multiple_of((me % groups) * cols, cols), cols), :]
    own_logit = split_dot(jnp.broadcast_to(own_sum, (8, cols)), own_class, 0)
    shower_id = lax.broadcasted_iota(jnp.int32, logit_part.shape, 0)
    logit_out[...] = logit_part + jnp.where(shower_id == own, own_logit[0:1, :], 0.0)

    def send_logit(step, carry):
        pltpu.make_async_remote_copy(
            src_ref=logit_out,
            dst_ref=logit_in.at[me],
            send_sem=logit_send,
            recv_sem=logit_recv,
            device_id={"head": lax.rem(me + step * STRIDE, n)},
            device_id_type=MESH,
        ).start()
        return carry

    pltpu.make_async_copy(logit_out, logit_in.at[me], logit_recv).start()
    lax.fori_loop(1, n, send_logit, 0)

    lax.fori_loop(0, chunks, finish, 0)
    row_of = lax.broadcasted_iota(jnp.int32, (rows_here, window_count), 0)
    slot_in = lax.broadcasted_iota(jnp.int32, (rows_here, window_count), 1)
    wanted = me * per_device + row_of % per_device
    own_count = jnp.zeros((rows_here, lanes), jnp.float32)
    for s in range(showers):
        select = jnp.where((row_of // per_device == s) & (slot_in == wanted), 1.0, 0.0).astype(
            jnp.bfloat16
        )
        own_count = own_count + jnp.dot(
            select, count_col[s].astype(jnp.bfloat16), preferred_element_type=jnp.float32
        )
        for j in range(groups):
            columns = pl.ds(j * cols, cols)
            picked = jnp.dot(
                select, gathered[s * groups + j], preferred_element_type=jnp.float32
            )
            own_pooled[:, columns] = picked if s == 0 else own_pooled[:, columns] + picked

    wait_whole(logit_in, logit_recv)
    total = logit_in[0]
    for source in range(1, n):
        total = total + logit_in[source]
    shower_counts = cnt[...].astype(jnp.float32)
    logits = total / shower_counts + bias[...]
    exponent = jnp.exp(logits - jnp.max(logits, axis=1, keepdims=True))
    probability = exponent / jnp.sum(exponent, axis=1, keepdims=True)
    target = jnp.where(
        labels[...] == lax.broadcasted_iota(jnp.int32, labels.shape, 1), 1.0, 0.0
    )
    feature_grad = split_dot(target - probability, class_w[...], 1)

    for s in range(showers):
        at = pl.ds(s * window_count, window_count)
        share = count_col[s][:, 0:1] / shower_counts[s : s + 1, 0:1]
        normed[at, :] = (share * feature_grad[s : s + 1, :]).astype(jnp.bfloat16)

    def backward(b, carry):
        at = pl.ds(pl.multiple_of(b * big, big), big)
        hidden_grad = lax.dot_general(
            normed[at, :], down[...], (((1,), (1,)), ((), ())), preferred_element_type=jnp.float32
        )
        dg_all[at, :] = (hidden_grad * u_all[at, :]).astype(jnp.bfloat16)
        du_all[at, :] = (hidden_grad * g_all[at, :]).astype(jnp.bfloat16)
        return carry

    lax.fori_loop(0, row_total // big, backward, 0)

    stream_width = width // streams

    def scatter_copy(stream, slot, bit, r):
        columns = pl.ds(stream * stream_width, stream_width)
        return pltpu.make_async_remote_copy(
            src_ref=x.at[flipped(r), :, columns],
            dst_ref=held.at[stream, slot],
            send_sem=rs_send.at[stream, slot],
            recv_sem=rs_recv.at[stream, slot],
            device_id={"head": flipped(1 << bit)},
            device_id_type=MESH,
        )

    everything = []
    quarter = n // 4
    part_rows = quarter * rows_here
    line = lax.broadcasted_iota(jnp.int32, (part_rows, row_total), 0)
    place = lax.broadcasted_iota(jnp.int32, (part_rows, row_total), 1)
    for base in (3, 1, 2, 0):
        chunk_of = lax.bitwise_xor(line // rows_here * 4 + base, jnp.full_like(line, me))
        within = line % rows_here
        source = (
            within // per_device * window_count + chunk_of * per_device + within % per_device
        )
        pick = jnp.where(source == place, 1.0, 0.0).astype(jnp.bfloat16)
        dg = jnp.dot(pick, dg_all[...], preferred_element_type=jnp.float32).astype(jnp.bfloat16)
        du = jnp.dot(pick, du_all[...], preferred_element_type=jnp.float32).astype(jnp.bfloat16)
        across = (((1,), (1,)), ((), ()))
        grad = lax.dot_general(dg, gate[...], across, preferred_element_type=jnp.float32)
        grad = grad + lax.dot_general(du, up[...], across, preferred_element_type=jnp.float32)
        grad = grad.astype(jnp.bfloat16)
        for p in range(quarter):
            r = 4 * p + base
            x[flipped(r)] = grad[p * rows_here : (p + 1) * rows_here]
            if base % 2:
                for stream, stages in enumerate(plan):
                    bit, away, kept = stages[0]
                    copy = scatter_copy(stream, away.index(r), bit, r)
                    copy.start()
                    everything.append(copy)

    stage_count = len(plan[0])
    slots = [0]
    for stage in range(stage_count):
        slots.append(slots[-1] + len(plan[0][stage][1]))
    for stage in range(stage_count):
        for i in range(len(plan[0][stage][1])):
            for stream, stages in enumerate(plan):
                bit, away, kept = stages[stage]
                slot = slots[stage] + i
                scatter_copy(stream, slot, bit, away[i]).wait_recv()
                columns = pl.ds(stream * stream_width, stream_width)
                chunk_id = flipped(kept[i])
                value = x[chunk_id, :, columns].astype(jnp.float32) + held[stream, slot].astype(
                    jnp.float32
                )
                if stage == stage_count - 1:
                    own_total[:, columns] = value
                    continue
                x[chunk_id, :, columns] = value.astype(jnp.bfloat16)
                next_bit, next_away, _ = stages[stage + 1]
                if kept[i] in next_away:
                    copy = scatter_copy(
                        stream,
                        slots[stage + 1] + next_away.index(kept[i]),
                        next_bit,
                        kept[i],
                    )
                    copy.start()
                    everything.append(copy)

    row_id = lax.broadcasted_iota(jnp.int32, (rows_here, 1), 0) // per_device

    def by_row(table):
        result = table[0]
        for s in range(1, showers):
            result = jnp.where(row_id == s, table[s], result)
        return result

    pooled = own_pooled[...]
    inverse = lax.rsqrt(jnp.sum(pooled * pooled, axis=1, keepdims=True) * (1.0 / width) + epsilon)
    units = pooled * inverse
    unit_grad = own_total[...] * by_row(scale_tab)
    inner = jnp.sum(unit_grad * units, axis=1, keepdims=True) * (1.0 / width)
    pooled_grad = inverse * (unit_grad - units * inner)
    share = own_count[:, 0:1] / by_row([shower_counts[s : s + 1, 0:1] for s in range(showers)])
    guidance[...] = window_count * (share * by_row([feature_grad[s : s + 1, :] for s in range(showers)]) + pooled_grad)

    wait_whole(logit_in.at[pl.ds(0, n - 1)], logit_send)
    for copy in everything:
        copy.wait_send()


def block(n, head_dim, cols, orders, collect_orders, operands):
    q, k, v, pos, cnt, labels, emb, gain, bias, time_w, gate, up, down, class_w = operands
    showers, rows, width = q.shape
    length = n * rows
    lanes = 2 * head_dim
    chunks = cols // lanes
    heads = cols // head_dim
    windows = length // POOL
    row_total = showers * windows
    rows_here = row_total // n
    hidden = gate.shape[1]
    streams = len(orders)
    moving = pltpu.VMEM((chunks, length, lanes), jnp.bfloat16)
    f32, b16, dma = jnp.float32, jnp.bfloat16, pltpu.SemaphoreType.DMA
    hbm, vmem = pl.BlockSpec(memory_space=pl.ANY), pl.BlockSpec(memory_space=pltpu.VMEM)
    return pl.pallas_call(
        functools.partial(block_kernel, n, head_dim, scatter_plan(n, orders), collect_orders),
        out_shape=(
            jax.ShapeDtypeStruct((heads, head_dim, length), b16),
            jax.ShapeDtypeStruct((rows_here, width), f32),
        ),
        in_specs=[hbm] * 3 + [vmem] * 6 + [hbm] * 5,
        out_specs=[hbm, vmem],
        scratch_shapes=[
            moving,
            moving,
            moving,
            pltpu.VMEM((2, 2 * lanes, length), b16),
            pltpu.VMEM((2, length, lanes), b16),
            pltpu.VMEM((heads, head_dim, length), b16),
            pltpu.VMEM((1, length), f32),
            pltpu.VMEM((length, lanes), f32),
            pltpu.VMEM((n,) + pos.shape, pos.dtype),
            pltpu.VMEM((n, windows, cols), b16),
            pltpu.VMEM((row_total, width), b16),
            pltpu.VMEM(gate.shape, b16),
            pltpu.VMEM(up.shape, b16),
            pltpu.VMEM(down.shape, b16),
            pltpu.VMEM(time_w.shape, b16),
            pltpu.VMEM(class_w.shape, b16),
            pltpu.VMEM((row_total, hidden), f32),
            pltpu.VMEM((row_total, hidden), f32),
            pltpu.VMEM((row_total, hidden), b16),
            pltpu.VMEM((row_total, hidden), b16),
            pltpu.VMEM((showers, windows, lanes), f32),
            pltpu.VMEM((showers, 1, width), f32),
            pltpu.VMEM((showers, 1, width), f32),
            pltpu.VMEM((n, showers, bias.shape[1]), f32),
            pltpu.VMEM((showers, bias.shape[1]), f32),
            pltpu.VMEM((rows_here, width), f32),
            pltpu.VMEM((rows_here, width), f32),
            pltpu.VMEM((n, rows_here, width), b16),
            pltpu.VMEM((streams, n, rows_here, width // streams), b16),
            dma((3, chunks)),
            dma((3, chunks)),
            dma,
            dma,
            dma((chunks,)),
            dma((5,)),
            dma((chunks, streams, n)),
            dma((chunks, streams, n)),
            dma,
            dma,
            dma((streams, n)),
            dma((streams, n)),
        ],
        compiler_params=pltpu.CompilerParams(
            collective_id=1, has_side_effects=True, vmem_limit_bytes=VMEM_MIB * 1024 * 1024
        ),
    )(*operands)


def body(
    queries,
    keys,
    values,
    slot_positions,
    counts,
    timesteps,
    labels,
    time_weight,
    norm_gain,
    gate_weight,
    up_weight,
    down_weight,
    class_weight,
    class_bias,
):
    devices = lax.axis_size("head")
    device_index = lax.axis_index("head")
    showers, local_length, model_width = queries.shape
    head_dim = model_width // HEADS
    cols = showers * model_width // devices
    lanes = 2 * head_dim
    per_lane_row = lanes // local_length
    positions = lax.dynamic_update_slice_in_dim(
        jnp.zeros((showers, lanes), jnp.int32),
        slot_positions,
        (device_index % per_lane_row) * local_length,
        1,
    )
    embedding = sinusoid(timesteps, time_weight.shape[0]).astype(jnp.bfloat16)
    bits = devices.bit_length() - 1
    high = list(range(3, bits))
    attention, guidance = block(
        devices,
        head_dim,
        cols,
        ([0, 1, 2] + high, [0, 2, 1] + high),
        (high + [2, 1, 0], high + [1, 2, 0]),
        (
            queries,
            keys,
            values,
            positions,
            jnp.broadcast_to(counts[:, None], (showers, lanes)),
            jnp.broadcast_to(labels[:, None], (showers, class_bias.shape[0])),
            embedding,
            norm_gain[None, :],
            class_bias[None, :],
            time_weight,
            gate_weight,
            up_weight,
            down_weight,
            class_weight,
        ),
    )
    per_device = guidance.shape[0] // showers
    return (attention.transpose(0, 2, 1), guidance.reshape(showers, per_device, model_width))


def solution(mesh):
    in_specs = (
        P("parts", "head", None),
        P("parts", "head", None),
        P("parts", "head", None),
        P("parts", "head"),
        P("parts"),
        P("parts"),
        P("parts"),
        P(),
        P(),
        P(None, "head"),
        P(None, "head"),
        P("head", None),
        P(),
        P(),
    )
    out_specs = (P(("parts", "head"), None, None), P("parts", "head", None))
    return jax.shard_map(body, mesh=mesh, in_specs=in_specs, out_specs=out_specs, check_vma=False)
```

```python
import functools
import math

import jax
import jax.numpy as jnp
from jax import lax
from jax.experimental import pallas as pl
from jax.experimental.pallas import tpu as pltpu
from jax.sharding import PartitionSpec as P

HEADS = 32
POOL = 16
QTILE = 256
AHEAD = 2
STRIDE = 11
VMEM_MIB = 60
FIRST_RELAY = 3
MESH = pl.DeviceIdType.MESH

epsilon = 1e-06


def sinusoid(steps, embed_width):
    half_width = embed_width // 2
    frequency = jnp.exp(-math.log(10000.0) * jnp.arange(half_width, dtype=jnp.float32) / half_width)
    angles = steps.astype(jnp.float32)[:, None] * frequency[None, :]
    return jnp.concatenate([jnp.cos(angles), jnp.sin(angles)], axis=1)


def greet_all(n, me):
    barrier = pltpu.get_barrier_semaphore()

    def greet(k, carry):
        pl.semaphore_signal(
            barrier, inc=1, device_id={"head": lax.rem(me + k, n)}, device_id_type=MESH
        )
        return carry

    lax.fori_loop(1, n, greet, 0)
    pl.semaphore_wait(barrier, n - 1)


def scatter_plan(n, orders):
    plan = []
    for order in orders:
        stages = []
        kept = list(range(n))
        for position, bit in enumerate(order):
            kept = [r for r in kept if not (r >> bit) & 1]
            following = order[position + 1] if position + 1 < len(order) else None
            if following is not None:
                kept.sort(key=lambda r: (1 - ((r >> following) & 1), r))
            away = [r ^ (1 << bit) for r in kept]
            stages.append((bit, away, list(kept)))
        plan.append(stages)
    return plan


def split_dot(x, matrix, contract):
    high = x.astype(jnp.bfloat16).astype(jnp.float32)
    middle = (x - high).astype(jnp.bfloat16).astype(jnp.float32)
    low = x - high - middle
    parts = jnp.concatenate([high, middle, low], axis=0).astype(jnp.bfloat16)
    result = lax.dot_general(
        parts, matrix, (((1,), (contract,)), ((), ())), preferred_element_type=jnp.float32
    )
    rows = x.shape[0]
    return result[:rows] + result[rows : 2 * rows] + result[2 * rows :]


def block_kernel(
    n, head_dim, plan, orders,
    q, k, v, pos, cnt, labels, emb, gain, bias, time_hbm, gate_hbm, up_hbm, down_hbm, class_hbm,
    att, guidance,
    qb, kb, vb, key_turned, mixed_in, att_held, bias_row, valid_col, everywhere,
    gathered, normed, gate, up, down, time_w, class_w,
    g_all, u_all, dg_all, du_all, count_col, shift_tab, scale_tab, logit_in, logit_out,
    own_pooled, own_total, x, held,
    send_sem, recv_sem, pos_send, pos_recv, out_sem, load_sem,
    ag_send, ag_recv, logit_send, logit_recv, rs_send, rs_recv,
):
    me = lax.axis_index("head")
    showers, rows, width = q.shape
    chunks, length, lanes = qb.shape
    cols = chunks * lanes
    groups = width // cols
    heads = lanes // head_dim
    per_lane_row = lanes // rows
    window_count = length // POOL
    per_device = window_count // n
    rows_here = showers * per_device
    row_total = showers * window_count
    bits = n.bit_length() - 1
    streams = len(orders)
    bit_of = [(me // (1 << b)) % 2 for b in range(bits)]
    fields = ((q, qb), (k, kb), (v, vb))

    def flipped(r):
        result = me
        for b in range(bits):
            if (r >> b) & 1:
                result = result + (1 << b) * (1 - 2 * bit_of[b])
        return result

    greet_all(n, me)

    def block_of(field, dst, c):
        start = pl.multiple_of((dst % groups) * cols + c * lanes, lanes)
        return field.at[dst // groups, :, pl.ds(start, lanes)]

    def slot_of(held, src, c):
        return held.at[c, pl.ds(pl.multiple_of(src * rows, rows), rows), :]

    def send_pos(step, carry):
        pltpu.make_async_remote_copy(
            src_ref=pos,
            dst_ref=everywhere.at[me],
            send_sem=pos_send,
            recv_sem=pos_recv,
            device_id={"head": lax.rem(me + step, n)},
            device_id_type=MESH,
        ).start()
        return carry

    pltpu.make_async_copy(pos, everywhere.at[me], pos_recv).start()
    lax.fori_loop(1, n, send_pos, 0)

    def send_chunk(c, carry):
        for i, (a, o) in enumerate(fields):
            pltpu.make_async_copy(block_of(a, me, c), slot_of(o, me, c), recv_sem.at[i, c]).start()

        def one(step, inner):
            dst = lax.rem(me + step * STRIDE, n)
            for i, (a, o) in enumerate(fields):
                pltpu.make_async_remote_copy(
                    src_ref=block_of(a, dst, c),
                    dst_ref=slot_of(o, me, c),
                    send_sem=send_sem.at[i, c],
                    recv_sem=recv_sem.at[i, c],
                    device_id={"head": dst},
                    device_id_type=MESH,
                ).start()
            return inner

        lax.fori_loop(1, n, one, 0)
        return carry

    ahead = min(AHEAD, chunks)
    lax.fori_loop(0, ahead, send_chunk, 0)

    loads = [
        pltpu.make_async_copy(a, o, load_sem.at[i])
        for i, (a, o) in enumerate(
            (
                (time_hbm, time_w),
                (gate_hbm, gate),
                (up_hbm, up),
                (down_hbm, down),
                (class_hbm, class_w),
            )
        )
    ]
    for load in loads:
        load.start()
    for load in loads:
        load.wait()
    modulation = jnp.dot(emb[...], time_w[...], preferred_element_type=jnp.float32)
    for s in range(showers):
        shift_tab[s] = modulation[s : s + 1, :width]
        scale_tab[s] = gain[...] * (1.0 + modulation[s : s + 1, width:])

    def wait_whole(ref, sem):
        pltpu.make_async_copy(ref, ref, sem).wait()

    wait_whole(everywhere, pos_recv)
    wait_whole(everywhere.at[pl.ds(0, n - 1)], pos_send)
    own = me // groups

    def valid_at(m, s):
        place = everywhere[m * per_lane_row, pl.ds(s, 1), :]
        for i in range(1, per_lane_row):
            place = place + everywhere[m * per_lane_row + i, pl.ds(s, 1), :]
        return place < cnt[pl.ds(s, 1), :]

    def mark(m, carry):
        valid = valid_at(m, own)
        at = pl.ds(pl.multiple_of(m * lanes, lanes), lanes)
        bias_row[:, at] = jnp.where(valid, 0.0, -1e30)
        wide = jnp.broadcast_to(jnp.where(valid, 1.0, 0.0), (lanes, lanes))
        valid_col[at, :] = wide.T
        return carry

    lax.fori_loop(0, length // lanes, mark, 0)

    per_row = lanes // POOL
    member = lax.broadcasted_iota(jnp.int32, (per_row, lanes), 0) == (
        lax.broadcasted_iota(jnp.int32, (per_row, lanes), 1) // POOL
    )

    def tally(m, carry):
        at = pl.ds(pl.multiple_of(m * per_row, per_row), per_row)
        for s in range(showers):
            picked = jnp.where(member & valid_at(m, s), 1.0, 0.0)
            count_col[s, at, :] = jnp.broadcast_to(
                jnp.sum(picked, axis=1, keepdims=True), (per_row, lanes)
            )
        return carry

    lax.fori_loop(0, length // lanes, tally, 0)

    height = window_count // streams

    last = (chunks - 1) * lanes
    spans = [(0, last)] * (chunks > 1) + [(last, lanes)]

    def gather_copy(span, stream, r, bit):
        part = gathered.at[
            flipped(r), pl.ds(stream * height, height), pl.ds(spans[span][0], spans[span][1])
        ]
        return pltpu.make_async_remote_copy(
            src_ref=part,
            dst_ref=part,
            send_sem=ag_send.at[span, stream, r | (1 << bit)],
            recv_sem=ag_recv.at[span, stream, r | (1 << bit)],
            device_id={"head": flipped(1 << bit)},
            device_id_type=MESH,
        )

    def gather_begin(span, stream):
        for bit in orders[stream]:
            gather_copy(span, stream, 0, bit).start()

    def had_before(order, stage):
        result = [0]
        for bit in order[:stage]:
            result += [r | (1 << bit) for r in result]
        return result

    def gather_relay(span, stream, stage):
        order = orders[stream]
        bit = order[stage]
        for r in had_before(order, stage):
            gather_copy(span, stream, r, bit).wait_recv()
            for later in order[stage + 1 :]:
                gather_copy(span, stream, r | (1 << bit), later).start()

    def gather_sent():
        for span in range(len(spans)):
            for stream, order in enumerate(orders):
                for stage, bit in enumerate(order):
                    for r in had_before(order, stage):
                        gather_copy(span, stream, r, bit).wait_send()

    qtile = min(QTILE, length)
    tiles = length // qtile
    kblock = min(512, length)
    lane = lax.broadcasted_iota(jnp.int32, (qtile, lanes), 1)
    windows = qtile // POOL
    window_row = lax.broadcasted_iota(jnp.int32, (windows, qtile), 0)
    window_slot = lax.broadcasted_iota(jnp.int32, (windows, qtile), 1)
    pool = jnp.where(window_slot // POOL == window_row, 1.0, 0.0).astype(jnp.bfloat16)
    factor = math.log2(math.e) * head_dim ** (-0.5)

    def chunk(c, carry):
        @pl.when(c + ahead < chunks)
        def _():
            send_chunk(c + ahead, 0)

        for i, (a, o) in enumerate(fields):
            wait_whole(o.at[c], recv_sem.at[i, c])

        def prepare(b, inner):
            at = pl.ds(pl.multiple_of(b * kblock, kblock), kblock)
            turned = kb[c, at, :].astype(jnp.float32).T
            row = lax.broadcasted_iota(jnp.int32, (lanes, kblock), 0)
            key_lane = lax.broadcasted_iota(jnp.int32, (kblock, lanes), 1)
            bias = bias_row[:, at]
            value = vb[c, at, :].astype(jnp.float32)
            for h in range(heads):
                spare = ((h + 1) % heads) * head_dim
                key_turned[h, 0:lanes, at] = turned.astype(jnp.bfloat16)
                key_turned[h, lanes : 2 * lanes, at] = jnp.where(row == spare, bias, turned).astype(
                    jnp.bfloat16
                )
                mixed_in[h, at, :] = jnp.where(key_lane == spare, 1.0, value).astype(jnp.bfloat16)
            return inner

        lax.fori_loop(0, length // kblock, prepare, 0)

        def tile(t, inner):
            if chunks > 1:

                @pl.when((c == chunks - 1) & (t == 0))
                def _():
                    for stream in range(streams):
                        gather_begin(0, stream)

                for stage in range(bits):

                    @pl.when((c == chunks - 1) & (t == FIRST_RELAY + stage))
                    def _():
                        for stream in range(streams):
                            gather_relay(0, stream, stage)

            at = pl.ds(pl.multiple_of(t * qtile, qtile), qtile)
            query = qb[c, at, :].astype(jnp.float32) * factor
            high = query.astype(jnp.bfloat16).astype(jnp.float32)
            low = query - high
            valid = valid_col[at, :]
            joined = None
            for h in range(heads):
                spare = ((h + 1) % heads) * head_dim
                inside = (lane >= h * head_dim) & (lane < (h + 1) * head_dim)
                both = jnp.concatenate(
                    [
                        jnp.where(inside, high, 0.0).astype(jnp.bfloat16),
                        jnp.where(inside, low, jnp.where(lane == spare, 1.0, 0.0)).astype(
                            jnp.bfloat16
                        ),
                    ],
                    axis=1,
                )
                scores = jnp.dot(both, key_turned[h], preferred_element_type=jnp.float32)
                peak = jnp.max(scores, axis=1, keepdims=True)
                weights = jnp.exp2(scores - peak).astype(jnp.bfloat16)
                result = jnp.dot(weights, mixed_in[h], preferred_element_type=jnp.float32)
                result = result * (valid / result[:, spare : spare + 1])
                joined = result if joined is None else jnp.where(inside, result, joined)
            turned = joined.T.astype(jnp.bfloat16)
            for h in range(heads):
                att_held[c * heads + h, :, at] = turned[h * head_dim : (h + 1) * head_dim, :]
            sums = jnp.dot(pool, joined.astype(jnp.bfloat16), preferred_element_type=jnp.float32)
            count = jnp.dot(pool, valid.astype(jnp.bfloat16), preferred_element_type=jnp.float32)
            gathered[
                me,
                pl.ds(pl.multiple_of(t * windows, windows), windows),
                pl.ds(pl.multiple_of(c * lanes, lanes), lanes),
            ] = (sums / jnp.maximum(count, 1.0)).astype(jnp.bfloat16)
            return inner

        lax.fori_loop(0, tiles, tile, 0)
        part = pl.ds(c * heads, heads)
        pltpu.make_async_copy(att_held.at[part], att.at[part], out_sem.at[c]).start()
        return carry

    lax.fori_loop(0, chunks, chunk, 0)
    for stream in range(streams):
        gather_begin(len(spans) - 1, stream)
    for stage in range(bits):
        for stream in range(streams):
            gather_relay(len(spans) - 1, stream, stage)

    def finish(c, carry):
        part = pl.ds(c * heads, heads)
        pltpu.make_async_copy(att_held.at[part], att.at[part], out_sem.at[c]).wait()
        for i, (a, o) in enumerate(fields):
            wait_whole(o.at[c, pl.ds(0, (n - 1) * rows)], send_sem.at[i, c])
        return carry

    def norm(s, carry):
        total = None
        for j in range(groups):
            part = gathered[s * groups + j].astype(jnp.float32)
            square = jnp.sum(part * part, axis=1, keepdims=True)
            total = square if total is None else total + square
        inverse = lax.rsqrt(total * (1.0 / width) + epsilon)
        at = pl.ds(pl.multiple_of(s * window_count, window_count), window_count)
        for j in range(groups):
            columns = pl.ds(j * cols, cols)
            part = gathered[s * groups + j].astype(jnp.float32)
            normed[at, columns] = (
                part * inverse * scale_tab[s, :, columns] + shift_tab[s, :, columns]
            ).astype(jnp.bfloat16)
        return carry

    lax.fori_loop(0, showers, norm, 0)

    big = min(512, row_total)

    def forward(b, carry):
        at = pl.ds(pl.multiple_of(b * big, big), big)
        part = normed[at, :]
        g_all[at, :] = jnp.dot(part, gate[...], preferred_element_type=jnp.float32)
        u_all[at, :] = jnp.dot(part, up[...], preferred_element_type=jnp.float32)
        return carry

    lax.fori_loop(0, row_total // big, forward, 0)

    hidden_sums = []
    for s in range(showers):
        at = pl.ds(s * window_count, window_count)
        g, u = g_all[at, :], u_all[at, :]
        sigma = 1.0 / (1.0 + jnp.exp(-g))
        active = g * sigma
        hidden = (active * u).astype(jnp.bfloat16).astype(jnp.float32)
        hidden_sums.append(jnp.sum(count_col[s][:, 0:1] * hidden, axis=0, keepdims=True))
        g_all[at, :] = active
        u_all[at, :] = u * sigma * (1.0 + g * (1.0 - sigma))
    mlp_sum = split_dot(jnp.concatenate(hidden_sums, axis=0), down[...], 0)
    logit_part = split_dot(mlp_sum, class_w[...], 0)
    own_sum = jnp.sum(
        count_col[own][:, 0:1] * gathered[me].astype(jnp.float32), axis=0, keepdims=True
    )
    own_class = class_w[pl.ds(pl.multiple_of((me % groups) * cols, cols), cols), :]
    own_logit = split_dot(jnp.broadcast_to(own_sum, (8, cols)), own_class, 0)
    shower_id = lax.broadcasted_iota(jnp.int32, logit_part.shape, 0)
    logit_out[...] = logit_part + jnp.where(shower_id == own, own_logit[0:1, :], 0.0)

    def send_logit(step, carry):
        pltpu.make_async_remote_copy(
            src_ref=logit_out,
            dst_ref=logit_in.at[me],
            send_sem=logit_send,
            recv_sem=logit_recv,
            device_id={"head": lax.rem(me + step * STRIDE, n)},
            device_id_type=MESH,
        ).start()
        return carry

    pltpu.make_async_copy(logit_out, logit_in.at[me], logit_recv).start()
    lax.fori_loop(1, n, send_logit, 0)

    lax.fori_loop(0, chunks, finish, 0)
    gather_sent()
    row_of = lax.broadcasted_iota(jnp.int32, (rows_here, window_count), 0)
    slot_in = lax.broadcasted_iota(jnp.int32, (rows_here, window_count), 1)
    wanted = me * per_device + row_of % per_device
    own_count = jnp.zeros((rows_here, lanes), jnp.float32)
    for s in range(showers):
        select = jnp.where((row_of // per_device == s) & (slot_in == wanted), 1.0, 0.0).astype(
            jnp.bfloat16
        )
        own_count = own_count + jnp.dot(
            select, count_col[s].astype(jnp.bfloat16), preferred_element_type=jnp.float32
        )
        for j in range(groups):
            columns = pl.ds(j * cols, cols)
            picked = jnp.dot(
                select, gathered[s * groups + j], preferred_element_type=jnp.float32
            )
            own_pooled[:, columns] = picked if s == 0 else own_pooled[:, columns] + picked

    wait_whole(logit_in, logit_recv)
    total = logit_in[0]
    for source in range(1, n):
        total = total + logit_in[source]
    shower_counts = cnt[...].astype(jnp.float32)
    logits = total / shower_counts + bias[...]
    exponent = jnp.exp(logits - jnp.max(logits, axis=1, keepdims=True))
    probability = exponent / jnp.sum(exponent, axis=1, keepdims=True)
    target = jnp.where(
        labels[...] == lax.broadcasted_iota(jnp.int32, labels.shape, 1), 1.0, 0.0
    )
    feature_grad = split_dot(target - probability, class_w[...], 1)

    for s in range(showers):
        at = pl.ds(s * window_count, window_count)
        share = count_col[s][:, 0:1] / shower_counts[s : s + 1, 0:1]
        normed[at, :] = (share * feature_grad[s : s + 1, :]).astype(jnp.bfloat16)

    def backward(b, carry):
        at = pl.ds(pl.multiple_of(b * big, big), big)
        hidden_grad = lax.dot_general(
            normed[at, :], down[...], (((1,), (1,)), ((), ())), preferred_element_type=jnp.float32
        )
        dg_all[at, :] = (hidden_grad * u_all[at, :]).astype(jnp.bfloat16)
        du_all[at, :] = (hidden_grad * g_all[at, :]).astype(jnp.bfloat16)
        return carry

    lax.fori_loop(0, row_total // big, backward, 0)

    stream_width = width // streams

    def scatter_copy(stream, slot, bit, r):
        columns = pl.ds(stream * stream_width, stream_width)
        return pltpu.make_async_remote_copy(
            src_ref=x.at[flipped(r), :, columns],
            dst_ref=held.at[stream, slot],
            send_sem=rs_send.at[stream, slot],
            recv_sem=rs_recv.at[stream, slot],
            device_id={"head": flipped(1 << bit)},
            device_id_type=MESH,
        )

    everything = []
    quarter = n // 4
    part_rows = quarter * rows_here
    line = lax.broadcasted_iota(jnp.int32, (part_rows, row_total), 0)
    place = lax.broadcasted_iota(jnp.int32, (part_rows, row_total), 1)
    for base in (3, 1, 2, 0):
        chunk_of = lax.bitwise_xor(line // rows_here * 4 + base, jnp.full_like(line, me))
        within = line % rows_here
        source = (
            within // per_device * window_count + chunk_of * per_device + within % per_device
        )
        pick = jnp.where(source == place, 1.0, 0.0).astype(jnp.bfloat16)
        dg = jnp.dot(pick, dg_all[...], preferred_element_type=jnp.float32).astype(jnp.bfloat16)
        du = jnp.dot(pick, du_all[...], preferred_element_type=jnp.float32).astype(jnp.bfloat16)
        across = (((1,), (1,)), ((), ()))
        grad = lax.dot_general(dg, gate[...], across, preferred_element_type=jnp.float32)
        grad = grad + lax.dot_general(du, up[...], across, preferred_element_type=jnp.float32)
        grad = grad.astype(jnp.bfloat16)
        for p in range(quarter):
            r = 4 * p + base
            x[flipped(r)] = grad[p * rows_here : (p + 1) * rows_here]
            if base % 2:
                for stream, stages in enumerate(plan):
                    bit, away, kept = stages[0]
                    copy = scatter_copy(stream, away.index(r), bit, r)
                    copy.start()
                    everything.append(copy)

    stage_count = len(plan[0])
    slots = [0]
    for stage in range(stage_count):
        slots.append(slots[-1] + len(plan[0][stage][1]))
    for stage in range(stage_count):
        for i in range(len(plan[0][stage][1])):
            for stream, stages in enumerate(plan):
                bit, away, kept = stages[stage]
                slot = slots[stage] + i
                scatter_copy(stream, slot, bit, away[i]).wait_recv()
                columns = pl.ds(stream * stream_width, stream_width)
                chunk_id = flipped(kept[i])
                value = x[chunk_id, :, columns].astype(jnp.float32) + held[stream, slot].astype(
                    jnp.float32
                )
                if stage == stage_count - 1:
                    own_total[:, columns] = value
                    continue
                x[chunk_id, :, columns] = value.astype(jnp.bfloat16)
                next_bit, next_away, _ = stages[stage + 1]
                if kept[i] in next_away:
                    copy = scatter_copy(
                        stream,
                        slots[stage + 1] + next_away.index(kept[i]),
                        next_bit,
                        kept[i],
                    )
                    copy.start()
                    everything.append(copy)

    row_id = lax.broadcasted_iota(jnp.int32, (rows_here, 1), 0) // per_device

    def by_row(table):
        result = table[0]
        for s in range(1, showers):
            result = jnp.where(row_id == s, table[s], result)
        return result

    pooled = own_pooled[...]
    inverse = lax.rsqrt(jnp.sum(pooled * pooled, axis=1, keepdims=True) * (1.0 / width) + epsilon)
    units = pooled * inverse
    unit_grad = own_total[...] * by_row(scale_tab)
    inner = jnp.sum(unit_grad * units, axis=1, keepdims=True) * (1.0 / width)
    pooled_grad = inverse * (unit_grad - units * inner)
    share = own_count[:, 0:1] / by_row([shower_counts[s : s + 1, 0:1] for s in range(showers)])
    guidance[...] = window_count * (share * by_row([feature_grad[s : s + 1, :] for s in range(showers)]) + pooled_grad)

    wait_whole(logit_in.at[pl.ds(0, n - 1)], logit_send)
    for copy in everything:
        copy.wait_send()


def block(n, head_dim, cols, orders, collect_orders, operands):
    q, k, v, pos, cnt, labels, emb, gain, bias, time_w, gate, up, down, class_w = operands
    showers, rows, width = q.shape
    length = n * rows
    lanes = 2 * head_dim
    chunks = cols // lanes
    heads = cols // head_dim
    windows = length // POOL
    row_total = showers * windows
    rows_here = row_total // n
    hidden = gate.shape[1]
    streams = len(orders)
    moving = pltpu.VMEM((chunks, length, lanes), jnp.bfloat16)
    f32, b16, dma = jnp.float32, jnp.bfloat16, pltpu.SemaphoreType.DMA
    hbm, vmem = pl.BlockSpec(memory_space=pl.ANY), pl.BlockSpec(memory_space=pltpu.VMEM)
    return pl.pallas_call(
        functools.partial(block_kernel, n, head_dim, scatter_plan(n, orders), collect_orders),
        out_shape=(
            jax.ShapeDtypeStruct((heads, head_dim, length), b16),
            jax.ShapeDtypeStruct((rows_here, width), f32),
        ),
        in_specs=[hbm] * 3 + [vmem] * 6 + [hbm] * 5,
        out_specs=[hbm, vmem],
        scratch_shapes=[
            moving,
            moving,
            moving,
            pltpu.VMEM((2, 2 * lanes, length), b16),
            pltpu.VMEM((2, length, lanes), b16),
            pltpu.VMEM((heads, head_dim, length), b16),
            pltpu.VMEM((1, length), f32),
            pltpu.VMEM((length, lanes), f32),
            pltpu.VMEM((n,) + pos.shape, pos.dtype),
            pltpu.VMEM((n, windows, cols), b16),
            pltpu.VMEM((row_total, width), b16),
            pltpu.VMEM(gate.shape, b16),
            pltpu.VMEM(up.shape, b16),
            pltpu.VMEM(down.shape, b16),
            pltpu.VMEM(time_w.shape, b16),
            pltpu.VMEM(class_w.shape, b16),
            pltpu.VMEM((row_total, hidden), f32),
            pltpu.VMEM((row_total, hidden), f32),
            pltpu.VMEM((row_total, hidden), b16),
            pltpu.VMEM((row_total, hidden), b16),
            pltpu.VMEM((showers, windows, lanes), f32),
            pltpu.VMEM((showers, 1, width), f32),
            pltpu.VMEM((showers, 1, width), f32),
            pltpu.VMEM((n, showers, bias.shape[1]), f32),
            pltpu.VMEM((showers, bias.shape[1]), f32),
            pltpu.VMEM((rows_here, width), f32),
            pltpu.VMEM((rows_here, width), f32),
            pltpu.VMEM((n, rows_here, width), b16),
            pltpu.VMEM((streams, n, rows_here, width // streams), b16),
            dma((3, chunks)),
            dma((3, chunks)),
            dma,
            dma,
            dma((chunks,)),
            dma((5,)),
            dma((2, streams, n)),
            dma((2, streams, n)),
            dma,
            dma,
            dma((streams, n)),
            dma((streams, n)),
        ],
        compiler_params=pltpu.CompilerParams(
            collective_id=1, has_side_effects=True, vmem_limit_bytes=VMEM_MIB * 1024 * 1024
        ),
    )(*operands)


def body(
    queries,
    keys,
    values,
    slot_positions,
    counts,
    timesteps,
    labels,
    time_weight,
    norm_gain,
    gate_weight,
    up_weight,
    down_weight,
    class_weight,
    class_bias,
):
    devices = lax.axis_size("head")
    device_index = lax.axis_index("head")
    showers, local_length, model_width = queries.shape
    head_dim = model_width // HEADS
    cols = showers * model_width // devices
    lanes = 2 * head_dim
    per_lane_row = lanes // local_length
    positions = lax.dynamic_update_slice_in_dim(
        jnp.zeros((showers, lanes), jnp.int32),
        slot_positions,
        (device_index % per_lane_row) * local_length,
        1,
    )
    embedding = sinusoid(timesteps, time_weight.shape[0]).astype(jnp.bfloat16)
    bits = devices.bit_length() - 1
    high = list(range(3, bits))
    attention, guidance = block(
        devices,
        head_dim,
        cols,
        ([0, 1, 2] + high, [0, 2, 1] + high),
        (high + [2, 1, 0], high + [1, 2, 0]),
        (
            queries,
            keys,
            values,
            positions,
            jnp.broadcast_to(counts[:, None], (showers, lanes)),
            jnp.broadcast_to(labels[:, None], (showers, class_bias.shape[0])),
            embedding,
            norm_gain[None, :],
            class_bias[None, :],
            time_weight,
            gate_weight,
            up_weight,
            down_weight,
            class_weight,
        ),
    )
    per_device = guidance.shape[0] // showers
    return (attention.transpose(0, 2, 1), guidance.reshape(showers, per_device, model_width))


def solution(mesh):
    in_specs = (
        P("parts", "head", None),
        P("parts", "head", None),
        P("parts", "head", None),
        P("parts", "head"),
        P("parts"),
        P("parts"),
        P("parts"),
        P(),
        P(),
        P(None, "head"),
        P(None, "head"),
        P("head", None),
        P(),
        P(),
    )
    out_specs = (P(("parts", "head"), None, None), P("parts", "head", None))
    return jax.shard_map(body, mesh=mesh, in_specs=in_specs, out_specs=out_specs, check_vma=False)
```

```python
import functools
import math

import jax
import jax.numpy as jnp
from jax import lax
from jax.experimental import pallas as pl
from jax.experimental.pallas import tpu as pltpu
from jax.sharding import PartitionSpec as P

HEADS = 32
POOL = 16
QTILE = 256
AHEAD = 2
STRIDE = 11
VMEM_MIB = 60
FIRST_RELAY = 3
EARLY = 2
MESH = pl.DeviceIdType.MESH

epsilon = 1e-06


def sinusoid(steps, embed_width):
    half_width = embed_width // 2
    frequency = jnp.exp(-math.log(10000.0) * jnp.arange(half_width, dtype=jnp.float32) / half_width)
    angles = steps.astype(jnp.float32)[:, None] * frequency[None, :]
    return jnp.concatenate([jnp.cos(angles), jnp.sin(angles)], axis=1)


def greet_all(n, me):
    barrier = pltpu.get_barrier_semaphore()

    def greet(k, carry):
        pl.semaphore_signal(
            barrier, inc=1, device_id={"head": lax.rem(me + k, n)}, device_id_type=MESH
        )
        return carry

    lax.fori_loop(1, n, greet, 0)
    pl.semaphore_wait(barrier, n - 1)


def scatter_plan(n, orders):
    plan = []
    for order in orders:
        stages = []
        kept = list(range(n))
        for position, bit in enumerate(order):
            kept = [r for r in kept if not (r >> bit) & 1]
            following = order[position + 1] if position + 1 < len(order) else None
            if following is not None:
                kept.sort(key=lambda r: (1 - ((r >> following) & 1), r))
            away = [r ^ (1 << bit) for r in kept]
            stages.append((bit, away, list(kept)))
        plan.append(stages)
    return plan


def split_dot(x, matrix, contract):
    high = x.astype(jnp.bfloat16).astype(jnp.float32)
    middle = (x - high).astype(jnp.bfloat16).astype(jnp.float32)
    low = x - high - middle
    parts = jnp.concatenate([high, middle, low], axis=0).astype(jnp.bfloat16)
    result = lax.dot_general(
        parts, matrix, (((1,), (contract,)), ((), ())), preferred_element_type=jnp.float32
    )
    rows = x.shape[0]
    return result[:rows] + result[rows : 2 * rows] + result[2 * rows :]


def block_kernel(
    n, head_dim, plan, orders,
    q, k, v, pos, cnt, labels, emb, gain, bias, time_hbm, gate_hbm, up_hbm, down_hbm, class_hbm,
    att, guidance,
    qb, kb, vb, key_turned, mixed_in, att_held, bias_row, valid_col, wide_pos, everywhere,
    gathered, normed, gate, up, down, time_w, class_w,
    g_all, u_all, dg_all, du_all, count_col, shift_tab, scale_tab, logit_in, logit_out,
    own_pooled, own_total, x, held,
    send_sem, recv_sem, pos_send, pos_recv, out_sem, load_sem,
    ag_send, ag_recv, logit_send, logit_recv, rs_send, rs_recv,
):
    me = lax.axis_index("head")
    showers, rows, width = q.shape
    chunks, length, lanes = qb.shape
    cols = chunks * lanes
    groups = width // cols
    heads = lanes // head_dim
    per_lane_row = lanes // rows
    window_count = length // POOL
    per_device = window_count // n
    rows_here = showers * per_device
    row_total = showers * window_count
    bits = n.bit_length() - 1
    streams = len(orders)
    bit_of = [(me // (1 << b)) % 2 for b in range(bits)]
    fields = ((q, qb), (k, kb), (v, vb))

    def flipped(r):
        result = me
        for b in range(bits):
            if (r >> b) & 1:
                result = result + (1 << b) * (1 - 2 * bit_of[b])
        return result

    greet_all(n, me)

    def block_of(field, dst, c):
        start = pl.multiple_of((dst % groups) * cols + c * lanes, lanes)
        return field.at[dst // groups, :, pl.ds(start, lanes)]

    def slot_of(held, src, c):
        return held.at[c, pl.ds(pl.multiple_of(src * rows, rows), rows), :]

    def send_pos(step, carry):
        pltpu.make_async_remote_copy(
            src_ref=wide_pos,
            dst_ref=everywhere.at[me],
            send_sem=pos_send,
            recv_sem=pos_recv,
            device_id={"head": lax.rem(me + step, n)},
            device_id_type=MESH,
        ).start()
        return carry

    lane_group = lax.broadcasted_iota(jnp.int32, (showers, lanes), 1) // rows
    wide_pos[...] = jnp.where(
        lane_group == me % per_lane_row, jnp.concatenate([pos[...]] * per_lane_row, axis=1), 0
    )
    pltpu.make_async_copy(wide_pos, everywhere.at[me], pos_recv).start()
    lax.fori_loop(1, n, send_pos, 0)

    def send_chunk(c, carry):
        for i, (a, o) in enumerate(fields):
            pltpu.make_async_copy(block_of(a, me, c), slot_of(o, me, c), recv_sem.at[i, c]).start()

        def one(step, inner):
            dst = lax.rem(me + step * STRIDE, n)
            for i, (a, o) in enumerate(fields):
                pltpu.make_async_remote_copy(
                    src_ref=block_of(a, dst, c),
                    dst_ref=slot_of(o, me, c),
                    send_sem=send_sem.at[i, c],
                    recv_sem=recv_sem.at[i, c],
                    device_id={"head": dst},
                    device_id_type=MESH,
                ).start()
            return inner

        lax.fori_loop(1, n, one, 0)
        return carry

    ahead = min(AHEAD, chunks)
    lax.fori_loop(0, ahead, send_chunk, 0)

    loads = [
        pltpu.make_async_copy(a, o, load_sem.at[i])
        for i, (a, o) in enumerate(
            (
                (time_hbm, time_w),
                (gate_hbm, gate),
                (up_hbm, up),
                (down_hbm, down),
                (class_hbm, class_w),
            )
        )
    ]
    for load in loads:
        load.start()
    for load in loads:
        load.wait()
    modulation = jnp.dot(emb[...], time_w[...], preferred_element_type=jnp.float32)
    for s in range(showers):
        shift_tab[s] = modulation[s : s + 1, :width]
        scale_tab[s] = gain[...] * (1.0 + modulation[s : s + 1, width:])

    def wait_whole(ref, sem):
        pltpu.make_async_copy(ref, ref, sem).wait()

    wait_whole(everywhere, pos_recv)
    wait_whole(everywhere.at[pl.ds(0, n - 1)], pos_send)
    own = me // groups

    def valid_at(m, s):
        place = everywhere[m * per_lane_row, pl.ds(s, 1), :]
        for i in range(1, per_lane_row):
            place = place + everywhere[m * per_lane_row + i, pl.ds(s, 1), :]
        return place < cnt[s]

    def mark(m, carry):
        valid = valid_at(m, own)
        at = pl.ds(pl.multiple_of(m * lanes, lanes), lanes)
        bias_row[:, at] = jnp.where(valid, 0.0, -1e30)
        wide = jnp.broadcast_to(jnp.where(valid, 1.0, 0.0), (lanes, lanes))
        valid_col[at, :] = wide.T
        return carry

    lax.fori_loop(0, length // lanes, mark, 0)

    per_row = lanes // POOL
    member = lax.broadcasted_iota(jnp.int32, (per_row, lanes), 0) == (
        lax.broadcasted_iota(jnp.int32, (per_row, lanes), 1) // POOL
    )

    def tally(m, carry):
        at = pl.ds(pl.multiple_of(m * per_row, per_row), per_row)
        for s in range(showers):
            picked = jnp.where(member & valid_at(m, s), 1.0, 0.0)
            count_col[s, at, :] = jnp.broadcast_to(
                jnp.sum(picked, axis=1, keepdims=True), (per_row, lanes)
            )
        return carry

    lax.fori_loop(0, length // lanes, tally, 0)

    height = window_count // streams

    last = (chunks - 1) * lanes
    final = int(chunks > 1)
    spans = [(0, last)] * (chunks > 1) + [(last, lanes)]

    def gather_copy(span, stream, r, bit):
        part = gathered.at[
            flipped(r), pl.ds(stream * height, height), pl.ds(spans[span][0], spans[span][1])
        ]
        return pltpu.make_async_remote_copy(
            src_ref=part,
            dst_ref=part,
            send_sem=ag_send.at[span, stream, r | (1 << bit)],
            recv_sem=ag_recv.at[span, stream, r | (1 << bit)],
            device_id={"head": flipped(1 << bit)},
            device_id_type=MESH,
        )

    def gather_begin(span, stream):
        for bit in orders[stream]:
            gather_copy(span, stream, 0, bit).start()

    def had_before(order, stage):
        result = [0]
        for bit in order[:stage]:
            result += [r | (1 << bit) for r in result]
        return result

    def gather_relay(span, stream, stage):
        order = orders[stream]
        bit = order[stage]
        for r in had_before(order, stage):
            gather_copy(span, stream, r, bit).wait_recv()
            for later in order[stage + 1 :]:
                gather_copy(span, stream, r | (1 << bit), later).start()

    def gather_sent():
        for span in range(len(spans)):
            for stream, order in enumerate(orders):
                for stage, bit in enumerate(order):
                    for r in had_before(order, stage):
                        gather_copy(span, stream, r, bit).wait_send()

    qtile = min(QTILE, length)
    tiles = length // qtile
    kblock = min(512, length)
    lane = lax.broadcasted_iota(jnp.int32, (qtile, lanes), 1)
    windows = qtile // POOL
    window_row = lax.broadcasted_iota(jnp.int32, (windows, qtile), 0)
    window_slot = lax.broadcasted_iota(jnp.int32, (windows, qtile), 1)
    pool = jnp.where(window_slot // POOL == window_row, 1.0, 0.0).astype(jnp.bfloat16)
    factor = math.log2(math.e) * head_dim ** (-0.5)

    def chunk(c, carry):
        @pl.when(c + ahead < chunks)
        def _():
            send_chunk(c + ahead, 0)

        for i, (a, o) in enumerate(fields):
            wait_whole(o.at[c], recv_sem.at[i, c])

        def prepare(b, inner):
            at = pl.ds(pl.multiple_of(b * kblock, kblock), kblock)
            turned = kb[c, at, :].astype(jnp.float32).T
            row = lax.broadcasted_iota(jnp.int32, (lanes, kblock), 0)
            key_lane = lax.broadcasted_iota(jnp.int32, (kblock, lanes), 1)
            bias = bias_row[:, at]
            value = vb[c, at, :].astype(jnp.float32)
            for h in range(heads):
                spare = ((h + 1) % heads) * head_dim
                key_turned[h, 0:lanes, at] = turned.astype(jnp.bfloat16)
                key_turned[h, lanes : 2 * lanes, at] = jnp.where(row == spare, bias, turned).astype(
                    jnp.bfloat16
                )
                mixed_in[h, at, :] = jnp.where(key_lane == spare, 1.0, value).astype(jnp.bfloat16)
            return inner

        lax.fori_loop(0, length // kblock, prepare, 0)

        def tile(t, inner):
            if chunks > 1:
                for stage in range(bits):

                    @pl.when((c == chunks - 1) & (t == FIRST_RELAY + stage))
                    def _():
                        for stream in range(streams):
                            gather_relay(0, stream, stage)

            @pl.when((c == chunks - 1) & (t == tiles // streams))
            def _():
                gather_begin(final, 0)

            for stage in range(EARLY):

                @pl.when((c == chunks - 1) & (t == tiles - EARLY + stage))
                def _():
                    gather_relay(final, 0, stage)

            at = pl.ds(pl.multiple_of(t * qtile, qtile), qtile)
            query = qb[c, at, :].astype(jnp.float32) * factor
            high = query.astype(jnp.bfloat16).astype(jnp.float32)
            low = query - high
            valid = valid_col[at, :]
            joined = None
            for h in range(heads):
                spare = ((h + 1) % heads) * head_dim
                inside = (lane >= h * head_dim) & (lane < (h + 1) * head_dim)
                both = jnp.concatenate(
                    [
                        jnp.where(inside, high, 0.0).astype(jnp.bfloat16),
                        jnp.where(inside, low, jnp.where(lane == spare, 1.0, 0.0)).astype(
                            jnp.bfloat16
                        ),
                    ],
                    axis=1,
                )
                scores = jnp.dot(both, key_turned[h], preferred_element_type=jnp.float32)
                peak = jnp.max(scores, axis=1, keepdims=True)
                weights = jnp.exp2(scores - peak).astype(jnp.bfloat16)
                result = jnp.dot(weights, mixed_in[h], preferred_element_type=jnp.float32)
                result = result * (valid / result[:, spare : spare + 1])
                joined = result if joined is None else jnp.where(inside, result, joined)
            turned = joined.T.astype(jnp.bfloat16)
            for h in range(heads):
                att_held[c * heads + h, :, at] = turned[h * head_dim : (h + 1) * head_dim, :]
            sums = jnp.dot(pool, joined.astype(jnp.bfloat16), preferred_element_type=jnp.float32)
            count = jnp.dot(pool, valid.astype(jnp.bfloat16), preferred_element_type=jnp.float32)
            gathered[
                me,
                pl.ds(pl.multiple_of(t * windows, windows), windows),
                pl.ds(pl.multiple_of(c * lanes, lanes), lanes),
            ] = (sums / jnp.maximum(count, 1.0)).astype(jnp.bfloat16)
            return inner

        lax.fori_loop(0, tiles, tile, 0)
        if chunks > 1:

            @pl.when(c == chunks - 2)
            def _():
                for stream in range(streams):
                    gather_begin(0, stream)

        part = pl.ds(c * heads, heads)
        pltpu.make_async_copy(att_held.at[part], att.at[part], out_sem.at[c]).start()
        return carry

    lax.fori_loop(0, chunks, chunk, 0)
    for stream in range(1, streams):
        gather_begin(final, stream)
    for stage in range(EARLY, bits + EARLY):
        if stage < bits:
            gather_relay(final, 0, stage)
        for stream in range(1, streams):
            gather_relay(final, stream, stage - EARLY)

    def finish(c, carry):
        part = pl.ds(c * heads, heads)
        pltpu.make_async_copy(att_held.at[part], att.at[part], out_sem.at[c]).wait()
        for i, (a, o) in enumerate(fields):
            wait_whole(o.at[c, pl.ds(0, (n - 1) * rows)], send_sem.at[i, c])
        return carry

    def norm(s, carry):
        total = None
        for j in range(groups):
            part = gathered[s * groups + j].astype(jnp.float32)
            square = jnp.sum(part * part, axis=1, keepdims=True)
            total = square if total is None else total + square
        inverse = lax.rsqrt(total * (1.0 / width) + epsilon)
        at = pl.ds(pl.multiple_of(s * window_count, window_count), window_count)
        for j in range(groups):
            columns = pl.ds(j * cols, cols)
            part = gathered[s * groups + j].astype(jnp.float32)
            normed[at, columns] = (
                part * inverse * scale_tab[s, :, columns] + shift_tab[s, :, columns]
            ).astype(jnp.bfloat16)
        return carry

    lax.fori_loop(0, showers, norm, 0)

    big = min(512, row_total)

    def forward(b, carry):
        at = pl.ds(pl.multiple_of(b * big, big), big)
        part = normed[at, :]
        g_all[at, :] = jnp.dot(part, gate[...], preferred_element_type=jnp.float32)
        u_all[at, :] = jnp.dot(part, up[...], preferred_element_type=jnp.float32)
        return carry

    lax.fori_loop(0, row_total // big, forward, 0)

    hidden_sums = []
    for s in range(showers):
        at = pl.ds(s * window_count, window_count)
        g, u = g_all[at, :], u_all[at, :]
        sigma = 1.0 / (1.0 + jnp.exp(-g))
        active = g * sigma
        hidden = (active * u).astype(jnp.bfloat16).astype(jnp.float32)
        hidden_sums.append(jnp.sum(count_col[s][:, 0:1] * hidden, axis=0, keepdims=True))
        g_all[at, :] = active
        u_all[at, :] = u * sigma * (1.0 + g * (1.0 - sigma))
    mlp_sum = split_dot(jnp.concatenate(hidden_sums, axis=0), down[...], 0)
    logit_part = split_dot(mlp_sum, class_w[...], 0)
    own_sum = jnp.sum(
        count_col[own][:, 0:1] * gathered[me].astype(jnp.float32), axis=0, keepdims=True
    )
    own_class = class_w[pl.ds(pl.multiple_of((me % groups) * cols, cols), cols), :]
    own_logit = split_dot(jnp.broadcast_to(own_sum, (8, cols)), own_class, 0)
    shower_id = lax.broadcasted_iota(jnp.int32, logit_part.shape, 0)
    logit_out[...] = logit_part + jnp.where(shower_id == own, own_logit[0:1, :], 0.0)

    def send_logit(step, carry):
        pltpu.make_async_remote_copy(
            src_ref=logit_out,
            dst_ref=logit_in.at[me],
            send_sem=logit_send,
            recv_sem=logit_recv,
            device_id={"head": lax.rem(me + step * STRIDE, n)},
            device_id_type=MESH,
        ).start()
        return carry

    pltpu.make_async_copy(logit_out, logit_in.at[me], logit_recv).start()
    lax.fori_loop(1, n, send_logit, 0)

    lax.fori_loop(0, chunks, finish, 0)
    gather_sent()
    row_of = lax.broadcasted_iota(jnp.int32, (rows_here, window_count), 0)
    slot_in = lax.broadcasted_iota(jnp.int32, (rows_here, window_count), 1)
    wanted = me * per_device + row_of % per_device
    own_count = jnp.zeros((rows_here, lanes), jnp.float32)
    for s in range(showers):
        select = jnp.where((row_of // per_device == s) & (slot_in == wanted), 1.0, 0.0).astype(
            jnp.bfloat16
        )
        own_count = own_count + jnp.dot(
            select, count_col[s].astype(jnp.bfloat16), preferred_element_type=jnp.float32
        )
        for j in range(groups):
            columns = pl.ds(j * cols, cols)
            picked = jnp.dot(
                select, gathered[s * groups + j], preferred_element_type=jnp.float32
            )
            own_pooled[:, columns] = picked if s == 0 else own_pooled[:, columns] + picked

    wait_whole(logit_in, logit_recv)
    total = logit_in[0]
    for source in range(1, n):
        total = total + logit_in[source]
    class_row = lax.broadcasted_iota(jnp.int32, total.shape, 0)
    shower_counts = jnp.zeros(total.shape, jnp.float32)
    label = jnp.zeros(total.shape, jnp.int32)
    for s in range(showers):
        shower_counts = jnp.where(class_row == s, cnt[s].astype(jnp.float32), shower_counts)
        label = jnp.where(class_row == s, labels[s], label)
    logits = total / shower_counts + bias[...]
    exponent = jnp.exp(logits - jnp.max(logits, axis=1, keepdims=True))
    probability = exponent / jnp.sum(exponent, axis=1, keepdims=True)
    target = jnp.where(
        label == lax.broadcasted_iota(jnp.int32, label.shape, 1), 1.0, 0.0
    )
    feature_grad = split_dot(target - probability, class_w[...], 1)

    for s in range(showers):
        at = pl.ds(s * window_count, window_count)
        share = count_col[s][:, 0:1] / shower_counts[s : s + 1, 0:1]
        normed[at, :] = (share * feature_grad[s : s + 1, :]).astype(jnp.bfloat16)

    def backward(b, carry):
        at = pl.ds(pl.multiple_of(b * big, big), big)
        hidden_grad = lax.dot_general(
            normed[at, :], down[...], (((1,), (1,)), ((), ())), preferred_element_type=jnp.float32
        )
        dg_all[at, :] = (hidden_grad * u_all[at, :]).astype(jnp.bfloat16)
        du_all[at, :] = (hidden_grad * g_all[at, :]).astype(jnp.bfloat16)
        return carry

    lax.fori_loop(0, row_total // big, backward, 0)

    stream_width = width // streams

    def scatter_copy(stream, slot, bit, r):
        columns = pl.ds(stream * stream_width, stream_width)
        return pltpu.make_async_remote_copy(
            src_ref=x.at[flipped(r), :, columns],
            dst_ref=held.at[stream, slot],
            send_sem=rs_send.at[stream, slot],
            recv_sem=rs_recv.at[stream, slot],
            device_id={"head": flipped(1 << bit)},
            device_id_type=MESH,
        )

    everything = []
    quarter = n // 4
    part_rows = quarter * rows_here
    line = lax.broadcasted_iota(jnp.int32, (part_rows, row_total), 0)
    place = lax.broadcasted_iota(jnp.int32, (part_rows, row_total), 1)
    for base in (3, 1, 2, 0):
        chunk_of = lax.bitwise_xor(line // rows_here * 4 + base, jnp.full_like(line, me))
        within = line % rows_here
        source = (
            within // per_device * window_count + chunk_of * per_device + within % per_device
        )
        pick = jnp.where(source == place, 1.0, 0.0).astype(jnp.bfloat16)
        dg = jnp.dot(pick, dg_all[...], preferred_element_type=jnp.float32).astype(jnp.bfloat16)
        du = jnp.dot(pick, du_all[...], preferred_element_type=jnp.float32).astype(jnp.bfloat16)
        across = (((1,), (1,)), ((), ()))
        grad = lax.dot_general(dg, gate[...], across, preferred_element_type=jnp.float32)
        grad = grad + lax.dot_general(du, up[...], across, preferred_element_type=jnp.float32)
        grad = grad.astype(jnp.bfloat16)
        for p in range(quarter):
            r = 4 * p + base
            x[flipped(r)] = grad[p * rows_here : (p + 1) * rows_here]
            if base % 2:
                for stream, stages in enumerate(plan):
                    bit, away, kept = stages[0]
                    copy = scatter_copy(stream, away.index(r), bit, r)
                    copy.start()
                    everything.append(copy)

    stage_count = len(plan[0])
    slots = [0]
    for stage in range(stage_count):
        slots.append(slots[-1] + len(plan[0][stage][1]))
    for stage in range(stage_count):
        for i in range(len(plan[0][stage][1])):
            for stream, stages in enumerate(plan):
                bit, away, kept = stages[stage]
                slot = slots[stage] + i
                scatter_copy(stream, slot, bit, away[i]).wait_recv()
                columns = pl.ds(stream * stream_width, stream_width)
                chunk_id = flipped(kept[i])
                value = x[chunk_id, :, columns].astype(jnp.float32) + held[stream, slot].astype(
                    jnp.float32
                )
                if stage == stage_count - 1:
                    own_total[:, columns] = value
                    continue
                x[chunk_id, :, columns] = value.astype(jnp.bfloat16)
                next_bit, next_away, _ = stages[stage + 1]
                if kept[i] in next_away:
                    copy = scatter_copy(
                        stream,
                        slots[stage + 1] + next_away.index(kept[i]),
                        next_bit,
                        kept[i],
                    )
                    copy.start()
                    everything.append(copy)

    row_id = lax.broadcasted_iota(jnp.int32, (rows_here, 1), 0) // per_device

    def by_row(table):
        result = table[0]
        for s in range(1, showers):
            result = jnp.where(row_id == s, table[s], result)
        return result

    pooled = own_pooled[...]
    inverse = lax.rsqrt(jnp.sum(pooled * pooled, axis=1, keepdims=True) * (1.0 / width) + epsilon)
    units = pooled * inverse
    unit_grad = own_total[...] * by_row(scale_tab)
    inner = jnp.sum(unit_grad * units, axis=1, keepdims=True) * (1.0 / width)
    pooled_grad = inverse * (unit_grad - units * inner)
    share = own_count[:, 0:1] / by_row([shower_counts[s : s + 1, 0:1] for s in range(showers)])
    row_grads = share * by_row([feature_grad[s : s + 1, :] for s in range(showers)])
    result = window_count * (row_grads + pooled_grad)
    for s in range(showers):
        guidance[s] = result[s * per_device : (s + 1) * per_device]

    wait_whole(logit_in.at[pl.ds(0, n - 1)], logit_send)
    for copy in everything:
        copy.wait_send()


def block(n, head_dim, cols, orders, collect_orders, operands):
    q, k, v, pos, cnt, labels, emb, gain, bias, time_w, gate, up, down, class_w = operands
    showers, rows, width = q.shape
    length = n * rows
    lanes = 2 * head_dim
    chunks = cols // lanes
    heads = cols // head_dim
    windows = length // POOL
    row_total = showers * windows
    rows_here = row_total // n
    hidden = gate.shape[1]
    streams = len(orders)
    moving = pltpu.VMEM((chunks, length, lanes), jnp.bfloat16)
    f32, b16, dma = jnp.float32, jnp.bfloat16, pltpu.SemaphoreType.DMA
    hbm, vmem = pl.BlockSpec(memory_space=pl.ANY), pl.BlockSpec(memory_space=pltpu.VMEM)
    smem = pl.BlockSpec(memory_space=pltpu.SMEM)
    return pl.pallas_call(
        functools.partial(block_kernel, n, head_dim, scatter_plan(n, orders), collect_orders),
        out_shape=(
            jax.ShapeDtypeStruct((heads, head_dim, length), b16),
            jax.ShapeDtypeStruct((showers, rows_here // showers, width), f32),
        ),
        in_specs=[hbm] * 3 + [vmem] + [smem] * 2 + [vmem] * 3 + [hbm] * 5,
        out_specs=[hbm, vmem],
        scratch_shapes=[
            moving,
            moving,
            moving,
            pltpu.VMEM((2, 2 * lanes, length), b16),
            pltpu.VMEM((2, length, lanes), b16),
            pltpu.VMEM((heads, head_dim, length), b16),
            pltpu.VMEM((1, length), f32),
            pltpu.VMEM((length, lanes), f32),
            pltpu.VMEM((showers, lanes), pos.dtype),
            pltpu.VMEM((n, showers, lanes), pos.dtype),
            pltpu.VMEM((n, windows, cols), b16),
            pltpu.VMEM((row_total, width), b16),
            pltpu.VMEM(gate.shape, b16),
            pltpu.VMEM(up.shape, b16),
            pltpu.VMEM(down.shape, b16),
            pltpu.VMEM(time_w.shape, b16),
            pltpu.VMEM(class_w.shape, b16),
            pltpu.VMEM((row_total, hidden), f32),
            pltpu.VMEM((row_total, hidden), f32),
            pltpu.VMEM((row_total, hidden), b16),
            pltpu.VMEM((row_total, hidden), b16),
            pltpu.VMEM((showers, windows, lanes), f32),
            pltpu.VMEM((showers, 1, width), f32),
            pltpu.VMEM((showers, 1, width), f32),
            pltpu.VMEM((n, showers, bias.shape[1]), f32),
            pltpu.VMEM((showers, bias.shape[1]), f32),
            pltpu.VMEM((rows_here, width), f32),
            pltpu.VMEM((rows_here, width), f32),
            pltpu.VMEM((n, rows_here, width), b16),
            pltpu.VMEM((streams, n, rows_here, width // streams), b16),
            dma((3, chunks)),
            dma((3, chunks)),
            dma,
            dma,
            dma((chunks,)),
            dma((5,)),
            dma((2, streams, n)),
            dma((2, streams, n)),
            dma,
            dma,
            dma((streams, n)),
            dma((streams, n)),
        ],
        compiler_params=pltpu.CompilerParams(
            collective_id=1, has_side_effects=True, vmem_limit_bytes=VMEM_MIB * 1024 * 1024
        ),
    )(*operands)


def hand_over_kernel(a, g, a_out, g_out):
    a_out[...] = a[...]
    g_out[...] = g[...]


def hand_over(a, g):
    steps = min(4, a.shape[0], g.shape[0])
    specs = [
        pl.BlockSpec((x.shape[0] // steps,) + x.shape[1:], lambda i: (i, 0, 0)) for x in (a, g)
    ]
    return pl.pallas_call(
        hand_over_kernel,
        grid=(steps,),
        out_shape=(jax.ShapeDtypeStruct(a.shape, a.dtype), jax.ShapeDtypeStruct(g.shape, g.dtype)),
        in_specs=specs,
        out_specs=specs,
    )(a, g)


def body(
    queries,
    keys,
    values,
    slot_positions,
    counts,
    timesteps,
    labels,
    time_weight,
    norm_gain,
    gate_weight,
    up_weight,
    down_weight,
    class_weight,
    class_bias,
):
    devices = lax.axis_size("head")
    showers, local_length, model_width = queries.shape
    head_dim = model_width // HEADS
    cols = showers * model_width // devices
    embedding = sinusoid(timesteps, time_weight.shape[0]).astype(jnp.bfloat16)
    bits = devices.bit_length() - 1
    high = list(range(3, bits))
    attention, guidance = block(
        devices,
        head_dim,
        cols,
        ([0, 1, 2] + high, [0] + high[:1] + [2, 1] + high[1:]),
        (high[::-1] + [2, 1, 0], high[::-1] + [1, 2, 0]),
        (
            queries,
            keys,
            values,
            slot_positions,
            counts,
            labels,
            embedding,
            norm_gain[None, :],
            class_bias[None, :],
            time_weight,
            gate_weight,
            up_weight,
            down_weight,
            class_weight,
        ),
    )
    attention, guidance = hand_over(attention, guidance)
    return (attention.transpose(0, 2, 1), guidance)


def solution(mesh):
    in_specs = (
        P("parts", "head", None),
        P("parts", "head", None),
        P("parts", "head", None),
        P("parts", "head"),
        P("parts"),
        P("parts"),
        P("parts"),
        P(),
        P(),
        P(None, "head"),
        P(None, "head"),
        P("head", None),
        P(),
        P(),
    )
    out_specs = (P(("parts", "head"), None, None), P("parts", "head", None))
    return jax.shard_map(body, mesh=mesh, in_specs=in_specs, out_specs=out_specs, check_vma=False)
```

```python
import functools
import math

import jax
import jax.numpy as jnp
from jax import lax
from jax.experimental import pallas as pl
from jax.experimental.pallas import tpu as pltpu
from jax.sharding import PartitionSpec as P

HEADS = 32
POOL = 16
QTILE = 256
AHEAD = 2
STRIDE = 11
VMEM_MIB = 60
FIRST_RELAY = 3
EARLY = 2
MESH = pl.DeviceIdType.MESH

epsilon = 1e-06


def sinusoid(steps, embed_width):
    half_width = embed_width // 2
    frequency = jnp.exp(-math.log(10000.0) * jnp.arange(half_width, dtype=jnp.float32) / half_width)
    angles = steps.astype(jnp.float32)[:, None] * frequency[None, :]
    return jnp.concatenate([jnp.cos(angles), jnp.sin(angles)], axis=1)


def greet_all(n, me):
    barrier = pltpu.get_barrier_semaphore()

    def greet(k, carry):
        pl.semaphore_signal(
            barrier, inc=1, device_id={"head": lax.rem(me + k, n)}, device_id_type=MESH
        )
        return carry

    lax.fori_loop(1, n, greet, 0)
    pl.semaphore_wait(barrier, n - 1)


def scatter_plan(n, orders):
    plan = []
    for order in orders:
        stages = []
        kept = list(range(n))
        for position, bit in enumerate(order):
            kept = [r for r in kept if not (r >> bit) & 1]
            following = order[position + 1] if position + 1 < len(order) else None
            if following is not None:
                kept.sort(key=lambda r: (1 - ((r >> following) & 1), r))
            away = [r ^ (1 << bit) for r in kept]
            stages.append((bit, away, list(kept)))
        plan.append(stages)
    return plan


def split_dot(x, matrix, contract):
    high = x.astype(jnp.bfloat16).astype(jnp.float32)
    middle = (x - high).astype(jnp.bfloat16).astype(jnp.float32)
    low = x - high - middle
    parts = jnp.concatenate([high, middle, low], axis=0).astype(jnp.bfloat16)
    result = lax.dot_general(
        parts, matrix, (((1,), (contract,)), ((), ())), preferred_element_type=jnp.float32
    )
    rows = x.shape[0]
    return result[:rows] + result[rows : 2 * rows] + result[2 * rows :]


def block_kernel(
    n, head_dim, plan, orders,
    q, k, v, pos, cnt, labels, emb, gain, bias, time_hbm, gate_hbm, up_hbm, down_hbm, class_hbm,
    att, guidance,
    qb, kb, vb, key_turned, mixed_in, att_held, bias_row, valid_col, wide_pos, everywhere,
    gathered, normed, gate, up, down, time_w, class_w,
    g_all, u_all, dg_all, du_all, count_col, shift_tab, scale_tab, logit_in, logit_out,
    own_pooled, own_total, x, held,
    send_sem, recv_sem, pos_send, pos_recv, out_sem, load_sem,
    ag_send, ag_recv, logit_send, logit_recv, rs_send, rs_recv,
):
    me = lax.axis_index("head")
    showers, rows, width = q.shape
    chunks, length, lanes = qb.shape
    cols = chunks * lanes
    groups = width // cols
    heads = lanes // head_dim
    per_lane_row = lanes // rows
    window_count = length // POOL
    per_device = window_count // n
    rows_here = showers * per_device
    row_total = showers * window_count
    bits = n.bit_length() - 1
    streams = len(orders)
    bit_of = [(me // (1 << b)) % 2 for b in range(bits)]
    fields = ((q, qb), (k, kb), (v, vb))

    def flipped(r):
        result = me
        for b in range(bits):
            if (r >> b) & 1:
                result = result + (1 << b) * (1 - 2 * bit_of[b])
        return result

    greet_all(n, me)

    def block_of(field, dst, c):
        start = pl.multiple_of((dst % groups) * cols + c * lanes, lanes)
        return field.at[dst // groups, :, pl.ds(start, lanes)]

    def slot_of(held, src, c):
        return held.at[c, pl.ds(pl.multiple_of(src * rows, rows), rows), :]

    def send_pos(step, carry):
        pltpu.make_async_remote_copy(
            src_ref=wide_pos,
            dst_ref=everywhere.at[me],
            send_sem=pos_send,
            recv_sem=pos_recv,
            device_id={"head": lax.rem(me + step, n)},
            device_id_type=MESH,
        ).start()
        return carry

    lane_group = lax.broadcasted_iota(jnp.int32, (showers, lanes), 1) // rows
    wide_pos[...] = jnp.where(
        lane_group == me % per_lane_row, jnp.concatenate([pos[...]] * per_lane_row, axis=1), 0
    )
    pltpu.make_async_copy(wide_pos, everywhere.at[me], pos_recv).start()
    lax.fori_loop(1, n, send_pos, 0)

    def send_chunk(c, carry):
        for i, (a, o) in enumerate(fields):
            pltpu.make_async_copy(block_of(a, me, c), slot_of(o, me, c), recv_sem.at[i, c]).start()

        def one(step, inner):
            dst = lax.rem(me + step * STRIDE, n)
            for i, (a, o) in enumerate(fields):
                pltpu.make_async_remote_copy(
                    src_ref=block_of(a, dst, c),
                    dst_ref=slot_of(o, me, c),
                    send_sem=send_sem.at[i, c],
                    recv_sem=recv_sem.at[i, c],
                    device_id={"head": dst},
                    device_id_type=MESH,
                ).start()
            return inner

        lax.fori_loop(1, n, one, 0)
        return carry

    ahead = min(AHEAD, chunks)
    lax.fori_loop(0, ahead, send_chunk, 0)

    loads = [
        pltpu.make_async_copy(a, o, load_sem.at[i])
        for i, (a, o) in enumerate(
            (
                (time_hbm, time_w),
                (gate_hbm, gate),
                (up_hbm, up),
                (down_hbm, down),
                (class_hbm, class_w),
            )
        )
    ]
    for load in loads:
        load.start()
    for load in loads:
        load.wait()
    modulation = jnp.dot(emb[...], time_w[...], preferred_element_type=jnp.float32)
    for s in range(showers):
        shift_tab[s] = modulation[s : s + 1, :width]
        scale_tab[s] = gain[...] * (1.0 + modulation[s : s + 1, width:])

    def wait_whole(ref, sem):
        pltpu.make_async_copy(ref, ref, sem).wait()

    wait_whole(everywhere, pos_recv)
    wait_whole(everywhere.at[pl.ds(0, n - 1)], pos_send)
    own = me // groups

    def valid_at(m, s):
        place = everywhere[m * per_lane_row, pl.ds(s, 1), :]
        for i in range(1, per_lane_row):
            place = place + everywhere[m * per_lane_row + i, pl.ds(s, 1), :]
        return place < cnt[s]

    def mark(m, carry):
        valid = valid_at(m, own)
        at = pl.ds(pl.multiple_of(m * lanes, lanes), lanes)
        bias_row[:, at] = jnp.where(valid, 0.0, -1e30)
        wide = jnp.broadcast_to(jnp.where(valid, 1.0, 0.0), (lanes, lanes))
        valid_col[at, :] = wide.T
        return carry

    lax.fori_loop(0, length // lanes, mark, 0)

    per_row = lanes // POOL
    member = lax.broadcasted_iota(jnp.int32, (per_row, lanes), 0) == (
        lax.broadcasted_iota(jnp.int32, (per_row, lanes), 1) // POOL
    )

    def tally(m, carry):
        at = pl.ds(pl.multiple_of(m * per_row, per_row), per_row)
        for s in range(showers):
            picked = jnp.where(member & valid_at(m, s), 1.0, 0.0)
            count_col[s, at, :] = jnp.broadcast_to(
                jnp.sum(picked, axis=1, keepdims=True), (per_row, lanes)
            )
        return carry

    lax.fori_loop(0, length // lanes, tally, 0)

    height = window_count // streams

    last = (chunks - 1) * lanes
    final = int(chunks > 1)
    spans = [(0, last)] * (chunks > 1) + [(last, lanes)]

    def gather_copy(span, stream, r, bit):
        part = gathered.at[
            flipped(r), pl.ds(stream * height, height), pl.ds(spans[span][0], spans[span][1])
        ]
        return pltpu.make_async_remote_copy(
            src_ref=part,
            dst_ref=part,
            send_sem=ag_send.at[span, stream, r | (1 << bit)],
            recv_sem=ag_recv.at[span, stream, r | (1 << bit)],
            device_id={"head": flipped(1 << bit)},
            device_id_type=MESH,
        )

    def gather_begin(span, stream):
        for bit in orders[stream]:
            gather_copy(span, stream, 0, bit).start()

    def had_before(order, stage):
        result = [0]
        for bit in order[:stage]:
            result += [r | (1 << bit) for r in result]
        return result

    def gather_relay(span, stream, stage):
        order = orders[stream]
        bit = order[stage]
        for r in had_before(order, stage):
            gather_copy(span, stream, r, bit).wait_recv()
            for later in order[stage + 1 :]:
                gather_copy(span, stream, r | (1 << bit), later).start()

    def gather_sent():
        for span in range(len(spans)):
            for stream, order in enumerate(orders):
                for stage, bit in enumerate(order):
                    for r in had_before(order, stage):
                        gather_copy(span, stream, r, bit).wait_send()

    qtile = min(QTILE, length)
    tiles = length // qtile
    kblock = min(512, length)
    lane = lax.broadcasted_iota(jnp.int32, (qtile, lanes), 1)
    windows = qtile // POOL
    window_row = lax.broadcasted_iota(jnp.int32, (windows, qtile), 0)
    window_slot = lax.broadcasted_iota(jnp.int32, (windows, qtile), 1)
    pool = jnp.where(window_slot // POOL == window_row, 1.0, 0.0).astype(jnp.bfloat16)
    factor = math.log2(math.e) * head_dim ** (-0.5)

    def chunk(c, carry):
        @pl.when(c + ahead < chunks)
        def _():
            send_chunk(c + ahead, 0)

        for i, (a, o) in enumerate(fields):
            wait_whole(o.at[c], recv_sem.at[i, c])

        def prepare(b, inner):
            at = pl.ds(pl.multiple_of(b * kblock, kblock), kblock)
            turned = kb[c, at, :].astype(jnp.float32).T
            row = lax.broadcasted_iota(jnp.int32, (lanes, kblock), 0)
            key_lane = lax.broadcasted_iota(jnp.int32, (kblock, lanes), 1)
            bias = bias_row[:, at]
            value = vb[c, at, :].astype(jnp.float32)
            for h in range(heads):
                spare = ((h + 1) % heads) * head_dim
                key_turned[h, 0:lanes, at] = turned.astype(jnp.bfloat16)
                key_turned[h, lanes : 2 * lanes, at] = jnp.where(row == spare, bias, turned).astype(
                    jnp.bfloat16
                )
                mixed_in[h, at, :] = jnp.where(key_lane == spare, 1.0, value).astype(jnp.bfloat16)
            return inner

        lax.fori_loop(0, length // kblock, prepare, 0)

        def tile(t, inner):
            if chunks > 1:
                for stage in range(bits):

                    @pl.when((c == chunks - 1) & (t == FIRST_RELAY + stage))
                    def _():
                        for stream in range(streams):
                            gather_relay(0, stream, stage)

            @pl.when((c == chunks - 1) & (t == tiles // streams))
            def _():
                gather_begin(final, 0)

            for stage in range(EARLY):

                @pl.when((c == chunks - 1) & (t == tiles - EARLY + stage))
                def _():
                    gather_relay(final, 0, stage)

            at = pl.ds(pl.multiple_of(t * qtile, qtile), qtile)
            query = qb[c, at, :].astype(jnp.float32) * factor
            high = query.astype(jnp.bfloat16).astype(jnp.float32)
            low = query - high
            valid = valid_col[at, :]
            joined = None
            for h in range(heads):
                spare = ((h + 1) % heads) * head_dim
                inside = (lane >= h * head_dim) & (lane < (h + 1) * head_dim)
                both = jnp.concatenate(
                    [
                        jnp.where(inside, high, 0.0).astype(jnp.bfloat16),
                        jnp.where(inside, low, jnp.where(lane == spare, 1.0, 0.0)).astype(
                            jnp.bfloat16
                        ),
                    ],
                    axis=1,
                )
                scores = jnp.dot(both, key_turned[h], preferred_element_type=jnp.float32)
                peak = jnp.max(scores, axis=1, keepdims=True)
                weights = jnp.exp2(scores - peak).astype(jnp.bfloat16)
                result = jnp.dot(weights, mixed_in[h], preferred_element_type=jnp.float32)
                result = result * (valid / result[:, spare : spare + 1])
                joined = result if joined is None else jnp.where(inside, result, joined)
            turned = joined.T.astype(jnp.bfloat16)
            for h in range(heads):
                att_held[c * heads + h, :, at] = turned[h * head_dim : (h + 1) * head_dim, :]
            sums = jnp.dot(pool, joined.astype(jnp.bfloat16), preferred_element_type=jnp.float32)
            count = jnp.dot(pool, valid.astype(jnp.bfloat16), preferred_element_type=jnp.float32)
            gathered[
                me,
                pl.ds(pl.multiple_of(t * windows, windows), windows),
                pl.ds(pl.multiple_of(c * lanes, lanes), lanes),
            ] = (sums / jnp.maximum(count, 1.0)).astype(jnp.bfloat16)
            return inner

        lax.fori_loop(0, tiles, tile, 0)
        if chunks > 1:

            @pl.when(c == chunks - 2)
            def _():
                for stream in range(streams):
                    gather_begin(0, stream)

        part = pl.ds(c * heads, heads)
        pltpu.make_async_copy(att_held.at[part], att.at[part], out_sem.at[c]).start()
        return carry

    lax.fori_loop(0, chunks, chunk, 0)
    for stream in range(1, streams):
        gather_begin(final, stream)
    for stage in range(EARLY, bits + EARLY):
        if stage < bits:
            gather_relay(final, 0, stage)
        for stream in range(1, streams):
            gather_relay(final, stream, stage - EARLY)

    def finish(c, carry):
        part = pl.ds(c * heads, heads)
        pltpu.make_async_copy(att_held.at[part], att.at[part], out_sem.at[c]).wait()
        for i, (a, o) in enumerate(fields):
            wait_whole(o.at[c, pl.ds(0, (n - 1) * rows)], send_sem.at[i, c])
        return carry

    def norm(s, carry):
        total = None
        for j in range(groups):
            part = gathered[s * groups + j].astype(jnp.float32)
            square = jnp.sum(part * part, axis=1, keepdims=True)
            total = square if total is None else total + square
        inverse = lax.rsqrt(total * (1.0 / width) + epsilon)
        at = pl.ds(pl.multiple_of(s * window_count, window_count), window_count)
        for j in range(groups):
            columns = pl.ds(j * cols, cols)
            part = gathered[s * groups + j].astype(jnp.float32)
            normed[at, columns] = (
                part * inverse * scale_tab[s, :, columns] + shift_tab[s, :, columns]
            ).astype(jnp.bfloat16)
        return carry

    lax.fori_loop(0, showers, norm, 0)

    big = min(512, row_total)

    def forward(b, carry):
        at = pl.ds(pl.multiple_of(b * big, big), big)
        part = normed[at, :]
        g_all[at, :] = jnp.dot(part, gate[...], preferred_element_type=jnp.float32)
        u_all[at, :] = jnp.dot(part, up[...], preferred_element_type=jnp.float32)
        return carry

    lax.fori_loop(0, row_total // big, forward, 0)

    hidden_sums = []
    for s in range(showers):
        at = pl.ds(s * window_count, window_count)
        g, u = g_all[at, :], u_all[at, :]
        sigma = 1.0 / (1.0 + jnp.exp(-g))
        active = g * sigma
        hidden = (active * u).astype(jnp.bfloat16).astype(jnp.float32)
        hidden_sums.append(jnp.sum(count_col[s][:, 0:1] * hidden, axis=0, keepdims=True))
        g_all[at, :] = active
        u_all[at, :] = u * sigma * (1.0 + g * (1.0 - sigma))
    mlp_sum = split_dot(jnp.concatenate(hidden_sums, axis=0), down[...], 0)
    logit_part = split_dot(mlp_sum, class_w[...], 0)
    own_sum = jnp.sum(
        count_col[own][:, 0:1] * gathered[me].astype(jnp.float32), axis=0, keepdims=True
    )
    own_class = class_w[pl.ds(pl.multiple_of((me % groups) * cols, cols), cols), :]
    own_logit = split_dot(jnp.broadcast_to(own_sum, (8, cols)), own_class, 0)
    shower_id = lax.broadcasted_iota(jnp.int32, logit_part.shape, 0)
    logit_out[...] = logit_part + jnp.where(shower_id == own, own_logit[0:1, :], 0.0)

    def send_logit(step, carry):
        pltpu.make_async_remote_copy(
            src_ref=logit_out,
            dst_ref=logit_in.at[me],
            send_sem=logit_send,
            recv_sem=logit_recv,
            device_id={"head": lax.rem(me + step * STRIDE, n)},
            device_id_type=MESH,
        ).start()
        return carry

    pltpu.make_async_copy(logit_out, logit_in.at[me], logit_recv).start()
    lax.fori_loop(1, n, send_logit, 0)

    lax.fori_loop(0, chunks, finish, 0)
    gather_sent()
    row_of = lax.broadcasted_iota(jnp.int32, (rows_here, window_count), 0)
    slot_in = lax.broadcasted_iota(jnp.int32, (rows_here, window_count), 1)
    wanted = me * per_device + row_of % per_device
    own_count = jnp.zeros((rows_here, lanes), jnp.float32)
    for s in range(showers):
        select = jnp.where((row_of // per_device == s) & (slot_in == wanted), 1.0, 0.0).astype(
            jnp.bfloat16
        )
        own_count = own_count + jnp.dot(
            select, count_col[s].astype(jnp.bfloat16), preferred_element_type=jnp.float32
        )
        for j in range(groups):
            columns = pl.ds(j * cols, cols)
            picked = jnp.dot(
                select, gathered[s * groups + j], preferred_element_type=jnp.float32
            )
            own_pooled[:, columns] = picked if s == 0 else own_pooled[:, columns] + picked

    wait_whole(logit_in, logit_recv)
    total = logit_in[0]
    for source in range(1, n):
        total = total + logit_in[source]
    class_row = lax.broadcasted_iota(jnp.int32, total.shape, 0)
    shower_counts = jnp.zeros(total.shape, jnp.float32)
    label = jnp.zeros(total.shape, jnp.int32)
    for s in range(showers):
        shower_counts = jnp.where(class_row == s, cnt[s].astype(jnp.float32), shower_counts)
        label = jnp.where(class_row == s, labels[s], label)
    logits = total / shower_counts + bias[...]
    exponent = jnp.exp(logits - jnp.max(logits, axis=1, keepdims=True))
    probability = exponent / jnp.sum(exponent, axis=1, keepdims=True)
    target = jnp.where(
        label == lax.broadcasted_iota(jnp.int32, label.shape, 1), 1.0, 0.0
    )
    feature_grad = split_dot(target - probability, class_w[...], 1)

    for s in range(showers):
        at = pl.ds(s * window_count, window_count)
        share = count_col[s][:, 0:1] / shower_counts[s : s + 1, 0:1]
        normed[at, :] = (share * feature_grad[s : s + 1, :]).astype(jnp.bfloat16)

    def backward(b, carry):
        at = pl.ds(pl.multiple_of(b * big, big), big)
        hidden_grad = lax.dot_general(
            normed[at, :], down[...], (((1,), (1,)), ((), ())), preferred_element_type=jnp.float32
        )
        dg_all[at, :] = (hidden_grad * u_all[at, :]).astype(jnp.bfloat16)
        du_all[at, :] = (hidden_grad * g_all[at, :]).astype(jnp.bfloat16)
        return carry

    lax.fori_loop(0, row_total // big, backward, 0)

    stream_width = width // streams

    def scatter_copy(stream, slot, bit, r):
        columns = pl.ds(stream * stream_width, stream_width)
        return pltpu.make_async_remote_copy(
            src_ref=x.at[flipped(r), :, columns],
            dst_ref=held.at[stream, slot],
            send_sem=rs_send.at[stream, slot],
            recv_sem=rs_recv.at[stream, slot],
            device_id={"head": flipped(1 << bit)},
            device_id_type=MESH,
        )

    everything = []
    quarter = n // 4
    part_rows = quarter * rows_here
    line = lax.broadcasted_iota(jnp.int32, (part_rows, row_total), 0)
    place = lax.broadcasted_iota(jnp.int32, (part_rows, row_total), 1)
    for base in (3, 1, 2, 0):
        chunk_of = lax.bitwise_xor(line // rows_here * 4 + base, jnp.full_like(line, me))
        within = line % rows_here
        source = (
            within // per_device * window_count + chunk_of * per_device + within % per_device
        )
        pick = jnp.where(source == place, 1.0, 0.0).astype(jnp.bfloat16)
        dg = jnp.dot(pick, dg_all[...], preferred_element_type=jnp.float32).astype(jnp.bfloat16)
        du = jnp.dot(pick, du_all[...], preferred_element_type=jnp.float32).astype(jnp.bfloat16)
        across = (((1,), (1,)), ((), ()))
        grad = lax.dot_general(dg, gate[...], across, preferred_element_type=jnp.float32)
        grad = grad + lax.dot_general(du, up[...], across, preferred_element_type=jnp.float32)
        grad = grad.astype(jnp.bfloat16)
        for p in range(quarter):
            r = 4 * p + base
            x[flipped(r)] = grad[p * rows_here : (p + 1) * rows_here]
            if base % 2:
                for stream, stages in enumerate(plan):
                    bit, away, kept = stages[0]
                    copy = scatter_copy(stream, away.index(r), bit, r)
                    copy.start()
                    everything.append(copy)

    stage_count = len(plan[0])
    slots = [0]
    for stage in range(stage_count):
        slots.append(slots[-1] + len(plan[0][stage][1]))
    for stage in range(stage_count):
        for i in range(len(plan[0][stage][1])):
            for stream, stages in enumerate(plan):
                bit, away, kept = stages[stage]
                slot = slots[stage] + i
                scatter_copy(stream, slot, bit, away[i]).wait_recv()
                columns = pl.ds(stream * stream_width, stream_width)
                chunk_id = flipped(kept[i])
                value = x[chunk_id, :, columns].astype(jnp.float32) + held[stream, slot].astype(
                    jnp.float32
                )
                if stage == stage_count - 1:
                    own_total[:, columns] = value
                    continue
                x[chunk_id, :, columns] = value.astype(jnp.bfloat16)
                next_bit, next_away, _ = stages[stage + 1]
                if kept[i] in next_away:
                    copy = scatter_copy(
                        stream,
                        slots[stage + 1] + next_away.index(kept[i]),
                        next_bit,
                        kept[i],
                    )
                    copy.start()
                    everything.append(copy)

    row_id = lax.broadcasted_iota(jnp.int32, (rows_here, 1), 0) // per_device

    def by_row(table):
        result = table[0]
        for s in range(1, showers):
            result = jnp.where(row_id == s, table[s], result)
        return result

    pooled = own_pooled[...]
    inverse = lax.rsqrt(jnp.sum(pooled * pooled, axis=1, keepdims=True) * (1.0 / width) + epsilon)
    units = pooled * inverse
    unit_grad = own_total[...] * by_row(scale_tab)
    inner = jnp.sum(unit_grad * units, axis=1, keepdims=True) * (1.0 / width)
    pooled_grad = inverse * (unit_grad - units * inner)
    share = own_count[:, 0:1] / by_row([shower_counts[s : s + 1, 0:1] for s in range(showers)])
    row_grads = share * by_row([feature_grad[s : s + 1, :] for s in range(showers)])
    result = window_count * (row_grads + pooled_grad)
    for s in range(showers):
        guidance[s] = result[s * per_device : (s + 1) * per_device]

    wait_whole(logit_in.at[pl.ds(0, n - 1)], logit_send)
    for copy in everything:
        copy.wait_send()


def block(n, head_dim, cols, orders, collect_orders, operands):
    q, k, v, pos, cnt, labels, emb, gain, bias, time_w, gate, up, down, class_w = operands
    showers, rows, width = q.shape
    length = n * rows
    lanes = 2 * head_dim
    chunks = cols // lanes
    heads = cols // head_dim
    windows = length // POOL
    row_total = showers * windows
    rows_here = row_total // n
    hidden = gate.shape[1]
    streams = len(orders)
    moving = pltpu.VMEM((chunks, length, lanes), jnp.bfloat16)
    f32, b16, dma = jnp.float32, jnp.bfloat16, pltpu.SemaphoreType.DMA
    hbm, vmem = pl.BlockSpec(memory_space=pl.ANY), pl.BlockSpec(memory_space=pltpu.VMEM)
    smem = pl.BlockSpec(memory_space=pltpu.SMEM)
    return pl.pallas_call(
        functools.partial(block_kernel, n, head_dim, scatter_plan(n, orders), collect_orders),
        out_shape=(
            jax.ShapeDtypeStruct((heads, head_dim, length), b16),
            jax.ShapeDtypeStruct((showers, rows_here // showers, width), f32),
        ),
        in_specs=[hbm] * 3 + [vmem] + [smem] * 2 + [vmem] * 3 + [hbm] * 5,
        out_specs=[hbm, vmem],
        scratch_shapes=[
            moving,
            moving,
            moving,
            pltpu.VMEM((2, 2 * lanes, length), b16),
            pltpu.VMEM((2, length, lanes), b16),
            pltpu.VMEM((heads, head_dim, length), b16),
            pltpu.VMEM((1, length), f32),
            pltpu.VMEM((length, lanes), f32),
            pltpu.VMEM((showers, lanes), pos.dtype),
            pltpu.VMEM((n, showers, lanes), pos.dtype),
            pltpu.VMEM((n, windows, cols), b16),
            pltpu.VMEM((row_total, width), b16),
            pltpu.VMEM(gate.shape, b16),
            pltpu.VMEM(up.shape, b16),
            pltpu.VMEM(down.shape, b16),
            pltpu.VMEM(time_w.shape, b16),
            pltpu.VMEM(class_w.shape, b16),
            pltpu.VMEM((row_total, hidden), f32),
            pltpu.VMEM((row_total, hidden), f32),
            pltpu.VMEM((row_total, hidden), b16),
            pltpu.VMEM((row_total, hidden), b16),
            pltpu.VMEM((showers, windows, lanes), f32),
            pltpu.VMEM((showers, 1, width), f32),
            pltpu.VMEM((showers, 1, width), f32),
            pltpu.VMEM((n, showers, bias.shape[1]), f32),
            pltpu.VMEM((showers, bias.shape[1]), f32),
            pltpu.VMEM((rows_here, width), f32),
            pltpu.VMEM((rows_here, width), f32),
            pltpu.VMEM((n, rows_here, width), b16),
            pltpu.VMEM((streams, n, rows_here, width // streams), b16),
            dma((3, chunks)),
            dma((3, chunks)),
            dma,
            dma,
            dma((chunks,)),
            dma((5,)),
            dma((2, streams, n)),
            dma((2, streams, n)),
            dma,
            dma,
            dma((streams, n)),
            dma((streams, n)),
        ],
        compiler_params=pltpu.CompilerParams(
            collective_id=1, has_side_effects=True, vmem_limit_bytes=VMEM_MIB * 1024 * 1024
        ),
    )(*operands)


def hand_over_kernel(a, g, a_out, g_out):
    a_out[...] = a[...]
    g_out[...] = g[...]


def hand_over(a, g):
    steps = min(2, a.shape[0], g.shape[0])
    specs = [
        pl.BlockSpec((x.shape[0] // steps,) + x.shape[1:], lambda i: (i, 0, 0)) for x in (a, g)
    ]
    return pl.pallas_call(
        hand_over_kernel,
        grid=(steps,),
        out_shape=(jax.ShapeDtypeStruct(a.shape, a.dtype), jax.ShapeDtypeStruct(g.shape, g.dtype)),
        in_specs=specs,
        out_specs=specs,
    )(a, g)


def body(
    queries,
    keys,
    values,
    slot_positions,
    counts,
    timesteps,
    labels,
    time_weight,
    norm_gain,
    gate_weight,
    up_weight,
    down_weight,
    class_weight,
    class_bias,
):
    devices = lax.axis_size("head")
    showers, local_length, model_width = queries.shape
    head_dim = model_width // HEADS
    cols = showers * model_width // devices
    embedding = sinusoid(timesteps, time_weight.shape[0]).astype(jnp.bfloat16)
    bits = devices.bit_length() - 1
    high = list(range(3, bits))
    attention, guidance = block(
        devices,
        head_dim,
        cols,
        ([0, 1, 2] + high, [0] + high[:1] + [2, 1] + high[1:]),
        (high[::-1] + [2, 1, 0], high[::-1] + [1, 2, 0]),
        (
            queries,
            keys,
            values,
            slot_positions,
            counts,
            labels,
            embedding,
            norm_gain[None, :],
            class_bias[None, :],
            time_weight,
            gate_weight,
            up_weight,
            down_weight,
            class_weight,
        ),
    )
    attention, guidance = hand_over(attention, guidance)
    return (attention.transpose(0, 2, 1), guidance)


def solution(mesh):
    in_specs = (
        P("parts", "head", None),
        P("parts", "head", None),
        P("parts", "head", None),
        P("parts", "head"),
        P("parts"),
        P("parts"),
        P("parts"),
        P(),
        P(),
        P(None, "head"),
        P(None, "head"),
        P("head", None),
        P(),
        P(),
    )
    out_specs = (P(("parts", "head"), None, None), P("parts", "head", None))
    return jax.shard_map(body, mesh=mesh, in_specs=in_specs, out_specs=out_specs, check_vma=False)
```
